32 devices in a mesh: dp: 4 (over y, x), mp: 8 (over z, core).
Axes of the slice: x: 2, y: 2, z: 4, core: 2. Of those that a mesh axis runs over, the one named last changes fastest.
Arguments:
- attn_input: bfloat16 [1024, 5120], P('dp'), may hold values from -8 to 8
- attn_gain: float32 [5120], replicated, may hold values from 0.1 to 1.9
- qkv_weight: float32 [5120, 6144], P(('dp', 'mp')), may hold values from -0.2 to 0.2
- mlp_input: bfloat16 [1024, 5120], P('dp'), may hold values from -6 to 6
- mlp_gain: float32 [5120], replicated, may hold values from 0.1 to 1.9
- gate_up_weight: float32 [5120, 32768], P(('dp', 'mp')), may hold values from -0.078125 to 0.078125
- prompt_lengths: int32 [6], replicated, may hold values from 1 to 512, 1024 in all
- request_prompt: int32 [64], replicated, may hold values from 0 to 5, as said below
- page_table: int32 [64, 4], replicated, may hold values from 0 to 383, as said below
Outputs:
- attended: bfloat16 [1024, 4096], P('dp', 'mp')
- hidden: bfloat16 [1024, 16384], P('dp', 'mp')
- kv_cache: bfloat16 [384, 128, 2048], P('dp', None, 'mp')
The draws below stay inside these ranges and needn't reach their ends.
Inputs may be any that keep to these rules, and one draw needn't show every extreme that they name: `prompt_lengths`: the lengths sum to 1024. `request_prompt`: each of the 6 prompts is named by 8 to 16 requests. `page_table`: all entries are distinct.
All inputs are finite; a program needn't handle non-finite values.
Results may differ from the reference program's by a relative error of at most 0.009.
Values may be sent and summed in bfloat16 or wider, within the bound.
No kernel may reach another device: no remote copies, remote signals or barrier semaphores. Data moves between devices by JAX's collectives and lax.ppermute only.
A program may use at most 192 MiB of HBM per device.

```python
import math
import jax
import jax.numpy as jnp
import numpy as np
from jax import lax

D = 5120
HEADS = 32
KVH = 8
HD = 128
FF = 16384
PROMPTS = 6
REQ = 64
PAGE = 128
TOKENS = 1024
LMAX = 512
PAGES_MAX = 4
QKVC = 6144
SLOTS = 384
N_MP = 8


def draw_attn_input(key, part):
    value = jnp.clip(jax.random.normal(jax.random.fold_in(key, 31), (TOKENS, D), jnp.float32), -6.0, 6.0)
    return value.astype(jnp.bfloat16)


def draw_qkv_weight(key, part):
    deviation = float(D) ** (-0.5)
    value = jnp.clip(jax.random.normal(jax.random.fold_in(key, 41), (D, QKVC), jnp.float32), -4.0, 4.0) * deviation
    return value.astype(jnp.float32)


def draw_request_prompt(key, part):
    counts = jnp.array([16, 8, 10, 10, 10, 10], dtype=jnp.int32)
    counts = jax.random.permutation(jax.random.fold_in(key, 11), counts)
    labels = jnp.repeat(jnp.arange(PROMPTS, dtype=jnp.int32), counts, total_repeat_length=REQ)
    return jax.random.permutation(jax.random.fold_in(key, 12), labels).astype(jnp.int32)


def draw_page_table(key, part):
    entry_count = REQ * PAGES_MAX
    middle_ids = jax.random.permutation(jax.random.fold_in(key, 13), SLOTS - 2)[:entry_count - 2] + 1
    chosen = jnp.concatenate([jnp.array([0, SLOTS - 1], dtype=jnp.int32), middle_ids.astype(jnp.int32)])
    return jax.random.permutation(jax.random.fold_in(key, 14), chosen).reshape(REQ, PAGES_MAX).astype(jnp.int32)


def level_of(stream_key, shape, split, least, top_value):
    def one(axis_at, blocks):
        draws = jax.random.uniform(jax.random.fold_in(jax.random.fold_in(stream_key, 6), axis_at), (blocks,), jnp.float32, least / len(split), top_value / len(split))
        return jnp.repeat(jnp.exp(draws), shape[axis_at] // blocks).reshape((-1,) + (1,) * (len(shape) - axis_at - 1))

    gain = one(*split[0])
    for cut in split[1:]:
        gain = gain * one(*cut)
    return gain


def profile(number_of, total, reach, lean):
    weights = [(1 << 20) // math.isqrt(grade ** lean) + 1 for grade in range(2, number_of + 1)]
    rest, holding = total - reach - (number_of - 1), [1] * (number_of - 1)
    while rest > 0:
        candidates = [i for i in range(number_of - 1) if holding[i] < reach]
        pool, remaining = sum([weights[i] for i in candidates]), rest
        for i in candidates:
            extra = min(reach - holding[i], max(1, remaining * weights[i] // pool), rest)
            holding[i] = holding[i] + extra
            rest = rest - extra
    return np.array([reach] + holding)


def ragged(own_key, amount, total, most, skew):
    if amount == 2:
        one = jax.random.randint(own_key, (), max(1, total - most), min(most, total - 1) + 1)
        return jnp.stack([one, total - one])
    sizes = jnp.asarray(profile(amount, total, most, skew), jnp.int32)
    twos = (amount - 1) // 2
    giver, receiver = sizes[1:1 + 2 * twos:2], sizes[2:2 + 2 * twos:2]
    room = jnp.minimum(giver - 1, most - receiver)
    shifted = jax.random.randint(jax.random.fold_in(own_key, 1), (twos,), 0, 1 << 20) % (room + 1)
    sizes = sizes.at[1:1 + 2 * twos:2].set(giver - shifted).at[2:2 + 2 * twos:2].set(receiver + shifted)
    return sizes[jax.random.permutation(jax.random.fold_in(own_key, 2), amount)]


def noise(rng, shape, scale, bound, split=(), kind=jnp.bfloat16):
    result = jax.random.normal(rng, shape, jnp.float32) * scale
    if len(split) > 0:
        result = level_of(rng, shape, split, -0.22, 0.18) * result
    return jnp.clip(result, min=-bound, max=bound).astype(kind)


def setup_inputs(seed: int = 0) -> dict:
    keys = jax.random.split(jax.random.key(seed), 10)
    return {
        "attn_input": draw_attn_input(jax.random.fold_in(keys[9], 71), 0),
        "attn_gain": jnp.clip(1.0 + 0.18 * jax.random.normal(keys[1], (D,), jnp.float32), 0.1, 1.9),
        "qkv_weight": draw_qkv_weight(jax.random.fold_in(keys[9], 71), 0),
        "mlp_input": noise(keys[3], (TOKENS, D), 1.0, 6.0, ((0, 4),)),
        "mlp_gain": jnp.clip(1.0 + 0.18 * jax.random.normal(keys[4], (D,), jnp.float32), 0.1, 1.9),
        "gate_up_weight": noise(keys[5], (D, 2 * FF), D ** -0.5, 0.078125, ((0, 32),), jnp.float32),
        "prompt_lengths": ragged(keys[6], PROMPTS, TOKENS, LMAX, 2).astype(jnp.int32),
        "request_prompt": draw_request_prompt(jax.random.fold_in(keys[9], 71), 0),
        "page_table": draw_page_table(jax.random.fold_in(keys[9], 71), 0),
    }


EPS = 1e-05
THETA = 100000000.0

def rms_norm(stream, gain_row):
    widened = stream.astype(jnp.float32)
    squares = lax.optimization_barrier(jnp.mean(widened * widened, axis=-1, keepdims=True))
    return (widened * lax.rsqrt(squares + EPS) * gain_row).astype(jnp.bfloat16)

def rotate(tensor, positions):
    half_dim = tensor.shape[-1] // 2
    frequency = THETA ** (-jnp.arange(half_dim, dtype=jnp.float32) / half_dim)
    angles = positions.astype(jnp.float32)[:, None] * frequency[None, :]
    cosine = jnp.cos(angles)[:, None, :]
    sine_part = jnp.sin(angles)[:, None, :]
    first_half = tensor[..., :half_dim]
    second_half = tensor[..., half_dim:]
    return jnp.concatenate([first_half * cosine - second_half * sine_part, second_half * cosine + first_half * sine_part], axis=-1)

def reference(attn_input, attn_gain, qkv_weight, mlp_input, mlp_gain, gate_up_weight, prompt_lengths, request_prompt, page_table):
    quarter_count = N_MP // KVH
    heads_here = HEADS // N_MP
    piece_dim = HD // quarter_count
    group_size = HEADS // KVH
    prompt_ends = jnp.cumsum(prompt_lengths).astype(jnp.int32)
    starts = prompt_ends - prompt_lengths
    token_ids = jnp.arange(TOKENS, dtype=jnp.int32)
    prompt_ids = lax.optimization_barrier(jnp.sum((token_ids[:, None] >= prompt_ends[None, :]).astype(jnp.int32), axis=1))
    positions = token_ids - starts[prompt_ids]
    normed = rms_norm(attn_input, attn_gain)
    projected = jnp.dot(normed, qkv_weight.astype(jnp.bfloat16), preferred_element_type=jnp.float32)
    query_cols = HEADS * HD
    queries = rotate(projected[:, :query_cols].reshape(TOKENS, HEADS, HD), positions).astype(jnp.bfloat16)
    key_heads = rotate(projected[:, query_cols:query_cols + KVH * HD].reshape(TOKENS, KVH, HD), positions).astype(jnp.bfloat16)
    value_heads = projected[:, query_cols + KVH * HD:].reshape(TOKENS, KVH, HD).astype(jnp.bfloat16)
    allowed = (prompt_ids[:, None] == prompt_ids[None, :]) & (token_ids[:, None] >= token_ids[None, :])

    def one_head(head_index):
        query_head = lax.dynamic_index_in_dim(queries, head_index, 1, keepdims=False)
        key_head = lax.dynamic_index_in_dim(key_heads, head_index // group_size, 1, keepdims=False)
        value_head = lax.dynamic_index_in_dim(value_heads, head_index // group_size, 1, keepdims=False)
        scores = jnp.dot(query_head, key_head.T, preferred_element_type=jnp.float32) * HD ** (-0.5)
        scores = jnp.where(allowed, scores, -jnp.inf)
        peak = lax.optimization_barrier(jnp.max(scores, axis=-1, keepdims=True))
        weights = jnp.exp(scores - peak)
        probs = (weights / lax.optimization_barrier(jnp.sum(weights, axis=-1, keepdims=True))).astype(jnp.bfloat16)
        return jnp.dot(probs, value_head, preferred_element_type=jnp.float32).astype(jnp.bfloat16)
    per_head = lax.map(one_head, jnp.arange(HEADS, dtype=jnp.int32))
    attended = per_head.reshape(KVH, quarter_count, heads_here, TOKENS, HD).transpose(3, 1, 0, 2, 4).reshape(TOKENS, HEADS * HD)
    entry_count = REQ * PAGES_MAX
    entries = jnp.arange(entry_count, dtype=jnp.int32)
    request_of = entries // PAGES_MAX
    page_of = entries % PAGES_MAX
    prompt_of = request_prompt[request_of]
    inside = page_of[:, None] * PAGE + jnp.arange(PAGE, dtype=jnp.int32)[None, :]
    valid = inside < prompt_lengths[prompt_of][:, None]
    source = jnp.where(valid, starts[prompt_of][:, None] + inside, 0)
    key_pages = key_heads[source].reshape(entry_count, PAGE, KVH, quarter_count, piece_dim)
    value_pages = value_heads[source].reshape(entry_count, PAGE, KVH, quarter_count, piece_dim)
    both_pages = jnp.stack([key_pages, value_pages], axis=4)
    both_pages = both_pages.transpose(0, 1, 3, 2, 4, 5).reshape(entry_count, PAGE, 2 * KVH * HD)
    both_pages = jnp.where(valid[:, :, None], both_pages, jnp.zeros((), jnp.bfloat16))
    kv_cache = jnp.zeros((SLOTS, PAGE, 2 * KVH * HD), jnp.bfloat16).at[page_table.reshape(-1)].set(both_pages)
    normed_mlp = rms_norm(mlp_input, mlp_gain)
    server_weight = gate_up_weight.astype(jnp.bfloat16)
    gate_sum = jnp.dot(normed_mlp, server_weight[:, :FF], preferred_element_type=jnp.float32)
    up_sum = jnp.dot(normed_mlp, server_weight[:, FF:], preferred_element_type=jnp.float32)
    hidden = (jax.nn.silu(gate_sum) * up_sum).astype(jnp.bfloat16)
    return (attended, hidden, kv_cache)
```

```python
import functools

import jax
import jax.numpy as jnp
from jax import lax
from jax.experimental import pallas as pl
from jax.experimental.pallas import tpu as pltpu
from jax.sharding import PartitionSpec as P

HEADS = 32
KVH = 8
HD = 128
PAGE = 128
EPS = 1e-05
THETA = 100000000.0
CHUNKS = 4
SLOT_DEV = 96
SLOT_GROUP = 8


def rms_norm(stream, gain_row):
    widened = stream.astype(jnp.float32)
    squares = jnp.mean(widened * widened, axis=-1, keepdims=True)
    return (widened * lax.rsqrt(squares + EPS) * gain_row).astype(jnp.bfloat16)


def rotate(tensor, positions):
    half_dim = tensor.shape[-1] // 2
    frequency = THETA ** (-jnp.arange(half_dim, dtype=jnp.float32) / half_dim)
    angles = positions.astype(jnp.float32)[:, None] * frequency[None, :]
    cosine = jnp.cos(angles)[:, None, :]
    sine_part = jnp.sin(angles)[:, None, :]
    first_half = tensor[..., :half_dim]
    second_half = tensor[..., half_dim:]
    return jnp.concatenate(
        [
            first_half * cosine - second_half * sine_part,
            second_half * cosine + first_half * sine_part,
        ],
        axis=-1,
    )


def swap(value, axis, offset):
    ways = lax.axis_size(axis)
    return lax.ppermute(value, axis, [(i, i ^ offset) for i in range(ways)])


def bits_of(ways):
    return [1 << i for i in range(ways.bit_length() - 1)]


def exchange_tokens(normed, rows):
    data_ways = lax.axis_size("dp")
    group = lax.axis_size("mp") // 2
    data_at, model_at = lax.axis_index("dp"), lax.axis_index("mp")
    tokens = normed.shape[0]
    half = lax.dynamic_index_in_dim(
        normed.reshape(tokens, data_ways, 2, group * rows), model_at // group, 2, keepdims=False
    )
    cells = half.reshape(tokens, data_ways, group, rows)
    for bit in bits_of(group):
        view = cells.reshape(tokens, data_ways, group // (2 * bit), 2, bit, rows)
        cells = jnp.where((model_at & bit) != 0, view[:, :, :, ::-1], view).reshape(cells.shape)
    cells = cells.transpose(1, 0, 2, 3).reshape(data_ways, tokens, group * rows)
    blocks = []
    for s in range(data_ways):
        block = lax.dynamic_index_in_dim(cells, data_at ^ s, 0, keepdims=False)
        blocks.append(block if s == 0 else swap(block, "dp", s))
    return blocks


def exchange_weights(pack):
    group = lax.axis_size("mp") // 2
    model_at = lax.axis_index("mp")
    side, member = model_at // group, model_at % group
    packets = []
    for s in range(group):
        packet = jnp.concatenate(
            [pack((side ^ a) * group + (member ^ s)) for a in range(2)], axis=1
        )
        packets.append(packet if s == 0 else swap(packet, "mp", s))
    width = packets[0].shape[1] // 2
    return [
        jnp.concatenate([packet[:, a * width : (a + 1) * width] for packet in packets], axis=0)
        for a in range(2)
    ]


def scattered_product(blocks, weights, order):
    arrived = {s: [] for s in range(len(blocks))}
    remaining = list(range(len(blocks)))

    def product(which):
        left = blocks[which[0]] if len(which) == 1 else jnp.concatenate([blocks[s] for s in which])
        total = jnp.dot(left, weights, preferred_element_type=jnp.float32)
        for parts in zip(*[arrived[s] for s in which]):
            joined = parts[0] if len(which) == 1 else jnp.concatenate(parts)
            total = total + joined.astype(jnp.float32)
        return total

    for bit in order:
        leaving = [s for s in remaining if s & bit]
        remaining = [s for s in remaining if not s & bit]
        received = swap(product(leaving).astype(jnp.bfloat16), "dp", bit)
        tokens = received.shape[0] // len(leaving)
        for i, s in enumerate(leaving):
            arrived[s ^ bit].append(received[i * tokens : (i + 1) * tokens])
    return product([0])


def projected(blocks, pack):
    own, other = exchange_weights(pack)
    order = bits_of(len(blocks))
    far = scattered_product(blocks, other, order[::-1]).astype(jnp.bfloat16)
    near = scattered_product(blocks, own, order)
    return near + swap(far, "mp", lax.axis_size("mp") // 2).astype(jnp.float32)


def feed_forward(blocks, gate_up_weight):
    ways = lax.axis_size("mp")
    half_cols = gate_up_weight.shape[1] // 2
    cols = half_cols // ways
    width = cols // CHUNKS
    pieces = []
    for chunk in range(CHUNKS):

        def pack(device):
            start = device * cols + chunk * width
            gate = lax.dynamic_slice_in_dim(gate_up_weight, start, width, 1)
            up = lax.dynamic_slice_in_dim(gate_up_weight, half_cols + start, width, 1)
            return jnp.concatenate([gate, up], axis=1).astype(jnp.bfloat16)

        both = projected(blocks, pack)
        pieces.append((jax.nn.silu(both[:, :width]) * both[:, width:]).astype(jnp.bfloat16))
    return jnp.concatenate(pieces, axis=1)


def attend_kernel(q_ref, k_ref, v_ref, first_ref, token_ref, out_ref):
    scores = lax.dot_general(
        q_ref[...], k_ref[...], (((1,), (1,)), ((), ())), preferred_element_type=jnp.float32
    ) * HD ** (-0.5)
    key_ids = lax.broadcasted_iota(jnp.int32, scores.shape, 1)
    allowed = (key_ids >= first_ref[...]) & (key_ids <= token_ref[...])
    scores = jnp.where(allowed, scores, -jnp.inf)
    peak = jnp.max(scores, axis=-1, keepdims=True)
    weights = jnp.exp(scores - peak)
    probs = (weights / jnp.sum(weights, axis=-1, keepdims=True)).astype(jnp.bfloat16)
    out_ref[...] = jnp.dot(probs, v_ref[...], preferred_element_type=jnp.float32).astype(jnp.bfloat16)


def attend(queries, keys, values, first, token):
    tokens, width = queries.shape
    total = keys.shape[0]
    heads = width // HD
    return pl.pallas_call(
        attend_kernel,
        grid=(heads,),
        in_specs=[
            pl.BlockSpec((tokens, HD), lambda h: (0, h)),
            pl.BlockSpec((total, HD), lambda h: (0, 0)),
            pl.BlockSpec((total, HD), lambda h: (0, 0)),
            pl.BlockSpec((tokens, 1), lambda h: (0, 0)),
            pl.BlockSpec((tokens, 1), lambda h: (0, 0)),
        ],
        out_specs=pl.BlockSpec((tokens, HD), lambda h: (0, h)),
        out_shape=jax.ShapeDtypeStruct((tokens, width), jnp.bfloat16),
        cost_estimate=pl.CostEstimate(
            flops=4 * tokens * total * width,
            transcendentals=tokens * total * heads,
            bytes_accessed=4 * tokens * width + 4 * total * HD,
        ),
        name="attend",
    )(queries, keys, values, first, token)


def pages_kernel(start_ref, count_ref, rows_ref, out_ref):
    group = out_ref.shape[0]
    base = pl.program_id(0) * group
    for i in range(group):
        start = start_ref[base + i]
        shift = lax.rem(start, 8)
        tall = rows_ref[pl.ds(pl.multiple_of(start - shift, 8), PAGE + 8), :]
        page = pltpu.roll(tall, lax.rem(PAGE + 8 - shift, PAGE + 8), 0)[:PAGE]
        inside = lax.broadcasted_iota(jnp.int32, page.shape, 0)
        out_ref[i] = jnp.where(inside < count_ref[base + i], page, 0.0).astype(jnp.bfloat16)


def fill_pages(rows, start, count):
    slots, width = start.shape[0], rows.shape[1]
    padded = jnp.concatenate(
        [rows.astype(jnp.float32), jnp.zeros((PAGE, width), jnp.float32)], axis=0
    )
    return pl.pallas_call(
        pages_kernel,
        grid_spec=pltpu.PrefetchScalarGridSpec(
            num_scalar_prefetch=2,
            grid=(slots // SLOT_GROUP,),
            in_specs=[pl.BlockSpec(padded.shape, lambda i, s, c: (0, 0))],
            out_specs=pl.BlockSpec((SLOT_GROUP, PAGE, width), lambda i, s, c: (i, 0, 0)),
        ),
        out_shape=jax.ShapeDtypeStruct((slots, PAGE, width), jnp.bfloat16),
        cost_estimate=pl.CostEstimate(
            flops=slots * PAGE * width,
            transcendentals=0,
            bytes_accessed=2 * slots * PAGE * width + 4 * padded.size,
        ),
        name="fill_pages",
    )(start, count, padded)


def page_sources(prompt_lengths, starts, request_prompt, page_table, slots):
    pages_per = page_table.shape[1]
    slot_ids = lax.axis_index("dp") * slots + jnp.arange(slots, dtype=jnp.int32)
    flat_table = page_table.reshape(-1)
    matches = slot_ids[:, None] == flat_table[None, :]
    is_used = jnp.any(matches, axis=1)
    entry_ids = jnp.sum(
        jnp.where(matches, jnp.arange(flat_table.shape[0], dtype=jnp.int32)[None, :], 0), axis=1
    )
    request_ids = entry_ids // pages_per
    offset = (entry_ids % pages_per) * PAGE
    request_match = (
        request_ids[:, None] == jnp.arange(request_prompt.shape[0], dtype=jnp.int32)[None, :]
    )
    prompt_pick = jnp.sum(jnp.where(request_match, request_prompt[None, :], 0), axis=1)
    prompt_match = (
        prompt_pick[:, None] == jnp.arange(prompt_lengths.shape[0], dtype=jnp.int32)[None, :]
    )
    slot_start = jnp.sum(jnp.where(prompt_match, starts[None, :], 0), axis=1)
    slot_length = jnp.sum(jnp.where(prompt_match, prompt_lengths[None, :], 0), axis=1)
    count = jnp.where(is_used, jnp.clip(slot_length - offset, 0, PAGE), 0)
    return jnp.where(count > 0, slot_start + offset, 0), count


def shards(
    attn_input,
    attn_gain,
    qkv_weight,
    mlp_input,
    mlp_gain,
    gate_up_weight,
    prompt_lengths,
    request_prompt,
    page_table,
    *,
    slots,
):
    model_ways = lax.axis_size("mp")
    quarter_count = model_ways // KVH
    heads_here = HEADS // model_ways
    piece_dim = HD // quarter_count
    tok_here = attn_input.shape[0]
    rows = qkv_weight.shape[0]
    query_width = heads_here * HD
    query_cols = HEADS * HD

    attn_blocks = exchange_tokens(rms_norm(attn_input, attn_gain), rows)
    mlp_blocks = exchange_tokens(rms_norm(mlp_input, mlp_gain), rows)

    def pack(device):
        kv_head, quarter = device % KVH, device // KVH
        query = lax.dynamic_slice_in_dim(
            qkv_weight, (kv_head * quarter_count + quarter) * query_width, query_width, 1
        )
        key = lax.dynamic_slice_in_dim(qkv_weight, query_cols + kv_head * HD, HD, 1)
        value = lax.dynamic_slice_in_dim(qkv_weight, query_cols + (KVH + kv_head) * HD, HD, 1)
        return jnp.concatenate([query, key, value], axis=1).astype(jnp.bfloat16)

    heads = projected(attn_blocks, pack).reshape(tok_here, heads_here + 2, HD)

    first_token = lax.axis_index("dp") * tok_here
    token_ids = first_token + jnp.arange(tok_here, dtype=jnp.int32)
    prompt_ends = jnp.cumsum(prompt_lengths)
    starts = prompt_ends - prompt_lengths
    begun = token_ids[:, None] >= starts[None, :]
    first = jnp.max(jnp.where(begun, starts[None, :], 0), axis=1)
    turned = rotate(heads[:, : heads_here + 1], token_ids - first).astype(jnp.bfloat16)
    queries = turned[:, :heads_here].reshape(tok_here, query_width)
    kv_local = jnp.concatenate(
        [turned[:, heads_here], heads[:, heads_here + 1].astype(jnp.bfloat16)], axis=1
    )
    kv_all = lax.all_gather(kv_local, "dp", axis=0, tiled=True)
    attended = attend(
        queries, kv_all[:, :HD], kv_all[:, HD:], first[:, None], token_ids[:, None]
    )
    piece_at = (lax.axis_index("mp") // KVH) * piece_dim
    page_rows = jnp.concatenate(
        [
            lax.dynamic_slice_in_dim(kv_all, piece_at, piece_dim, 1),
            lax.dynamic_slice_in_dim(kv_all, HD + piece_at, piece_dim, 1),
        ],
        axis=1,
    )
    kv_cache = fill_pages(
        page_rows, *page_sources(prompt_lengths, starts, request_prompt, page_table, slots)
    )
    hidden = feed_forward(mlp_blocks, gate_up_weight)
    return (attended, hidden, kv_cache)


def solution(mesh):
    data_ways = mesh.shape["dp"]
    placed = (
        P("dp", None),
        P(),
        P(("dp", "mp"), None),
        P("dp", None),
        P(),
        P(("dp", "mp"), None),
        P(),
        P(),
        P(),
    )

    def run(*args):
        return jax.shard_map(
            functools.partial(shards, slots=SLOT_DEV),
            mesh=mesh,
            in_specs=placed,
            out_specs=(P("dp", "mp"), P("dp", "mp"), P("dp", None, "mp")),
            check_vma=False,
        )(*args)

    return run
```

```python
import functools

import jax
import jax.numpy as jnp
from jax import lax
from jax.experimental import pallas as pl
from jax.experimental.pallas import tpu as pltpu
from jax.sharding import PartitionSpec as P

HEADS = 32
KVH = 8
HD = 128
PAGE = 128
EPS = 1e-05
THETA = 100000000.0
SLOT_DEV = 96
SLOT_GROUP = 8
SMALL = pl.CostEstimate(flops=1, transcendentals=0, bytes_accessed=1)


def rms_norm(stream, gain_row):
    widened = stream.astype(jnp.float32)
    squares = jnp.mean(widened * widened, axis=-1, keepdims=True)
    return (widened * lax.rsqrt(squares + EPS) * gain_row).astype(jnp.bfloat16)


def swap(value, axis, offset):
    ways = lax.axis_size(axis)
    return lax.ppermute(value, axis, [(i, i ^ offset) for i in range(ways)])


def bits_of(ways):
    return [1 << i for i in range(ways.bit_length() - 1)]


def member_order(group):
    return [*range(0, group, 2), *range(1, group, 2)]


def token_cells(streams, gains, rows):
    data_ways = lax.axis_size("dp")
    group = lax.axis_size("mp") // 2
    data_at, model_at = lax.axis_index("dp"), lax.axis_index("mp")
    cells = []
    for stream, gain_row in zip(streams, gains):
        tokens = stream.shape[0]
        half = lax.dynamic_index_in_dim(
            rms_norm(stream, gain_row).reshape(tokens, data_ways, 2, group, rows),
            model_at // group,
            2,
            keepdims=False,
        )
        members = jnp.array(member_order(group), dtype=jnp.int32) ^ (model_at % group)
        half = jnp.take(half, members, axis=2).transpose(1, 0, 2, 3)
        cells.append(half.reshape(data_ways, tokens, group * rows))
    own = [lax.dynamic_index_in_dim(cell, data_at, 0, keepdims=False) for cell in cells]
    both = jnp.concatenate(cells, axis=1)
    away = [
        lax.dynamic_index_in_dim(both, data_at ^ s, 0, keepdims=False) for s in range(1, data_ways)
    ]
    return [*own, *away]


def token_kernel(at_ref, *refs, group, rows, streams):
    data_at, side, member = at_ref[0], at_ref[1], at_ref[2]
    width = group * rows
    own_refs = refs[2 * streams : 3 * streams]
    away_refs = refs[3 * streams :]
    for k in range(streams):
        stream_ref, gain_ref = refs[k], refs[streams + k]
        tokens = stream_ref.shape[0]
        widened = stream_ref[...].astype(jnp.float32)
        scale = lax.rsqrt(jnp.mean(widened * widened, axis=-1, keepdims=True) + EPS)
        for s in range(len(away_refs) + 1):
            start = pl.multiple_of(((data_at ^ s) * 2 + side) * width, 128)
            block = stream_ref[:, pl.ds(start, width)].astype(jnp.float32)
            block = block * scale * gain_ref[:, pl.ds(start, width)]
            pieces = [block[:, i * rows : (i + 1) * rows] for i in range(group)]
            for bit in bits_of(group):
                pieces = [
                    jnp.where((member & bit) != 0, pieces[i ^ bit], pieces[i]) for i in range(group)
                ]
            block = jnp.concatenate([pieces[i] for i in member_order(group)], axis=1)
            block = block.astype(jnp.bfloat16)
            if s == 0:
                own_refs[k][...] = block
            else:
                away_refs[s - 1][k * tokens : (k + 1) * tokens, :] = block


def token_cells_kernel(streams, gains, rows):
    data_ways = lax.axis_size("dp")
    group = lax.axis_size("mp") // 2
    tokens, depth = streams[0].shape
    count = len(streams)
    model_at = lax.axis_index("mp")
    at = jnp.stack([lax.axis_index("dp"), model_at // group, model_at % group]).astype(jnp.int32)
    outs = [(tokens, group * rows)] * count
    outs += [(count * tokens, group * rows)] * (data_ways - 1)
    return pl.pallas_call(
        functools.partial(token_kernel, group=group, rows=rows, streams=count),
        grid_spec=pltpu.PrefetchScalarGridSpec(
            num_scalar_prefetch=1,
            grid=(1,),
            in_specs=[pl.BlockSpec((tokens, depth), lambda i, at: (0, 0))] * count
            + [pl.BlockSpec((1, depth), lambda i, at: (0, 0))] * count,
            out_specs=[pl.BlockSpec(shape, lambda i, at: (0, 0)) for shape in outs],
        ),
        out_shape=[jax.ShapeDtypeStruct(shape, jnp.bfloat16) for shape in outs],
        cost_estimate=SMALL,
        name="token_cells",
    )(at, *streams, *[gain_row[None] for gain_row in gains])


class Tokens:
    def __init__(self, order, streams, gains, rows):
        aligned = (lax.axis_size("mp") // 2 * rows) % 128 == 0
        streams = order.tie(*streams)
        cells = (token_cells_kernel if aligned else token_cells)(streams, gains, rows)
        self.order, self.own = order, cells[: len(streams)]
        order.last = self.own[0]
        self.away = [swap(cell, "dp", s + 1) for s, cell in enumerate(cells[len(streams) :])]

    def blocks(self):
        away = self.order.tie(*self.away)
        tokens = self.own[0].shape[0]
        return [
            [own, *[block[k * tokens : (k + 1) * tokens] for block in away]]
            for k, own in enumerate(self.own)
        ]


def copy_kernel(at_ref, *refs, members):
    for s in range(members):
        refs[members + s % 2][s // 2] = refs[s][...].astype(jnp.bfloat16)


def pack_columns(weight, starts, width):
    group = lax.axis_size("mp") // 2
    rows = weight.shape[0]
    count = len(starts)

    def spec(s):
        def place(i, at):
            device = ((at[0] // group) ^ (i % (2 * parts) // parts)) * group + ((at[0] % group) ^ s)
            column = starts[0](device)
            which = i // (2 * parts) * parts + i % parts
            for k in range(1, count):
                column = jnp.where(which == k, starts[k](device), column)
            return 0, pl.multiple_of(column, 128)

        return pl.BlockSpec((pl.Element(rows), pl.Element(width)), place)

    parts = 2 if count % 2 == 0 else 1
    steps = 2 * count
    out = jax.ShapeDtypeStruct((group // 2, rows, steps * width), jnp.bfloat16)
    return pl.pallas_call(
        functools.partial(copy_kernel, members=group),
        grid_spec=pltpu.PrefetchScalarGridSpec(
            num_scalar_prefetch=1,
            grid=(steps,),
            in_specs=[spec(s) for s in range(group)],
            out_specs=[pl.BlockSpec((group // 2, rows, width), lambda i, at: (0, 0, i))] * 2,
        ),
        out_shape=[out] * 2,
        cost_estimate=SMALL,
        name="pack_columns",
    )(lax.axis_index("mp")[None].astype(jnp.int32), *[weight] * group)


def heads_copy_kernel(at_ref, *refs, members, parts):
    for s in range(members):
        done = 0
        for p in range(parts):
            block = refs[s * parts + p][...].astype(jnp.bfloat16)
            refs[members * parts + s % 2][s // 2, :, done : done + block.shape[1]] = block
            done += block.shape[1]


def pack_heads(weight, head_starts):
    group = lax.axis_size("mp") // 2
    rows = weight.shape[0]
    heads = len(head_starts(0))
    widths = [(heads - 2) * HD, HD, HD]

    def spec(s, part):
        def place(i, at):
            device = ((at[0] // group) ^ i) * group + ((at[0] % group) ^ s)
            found = head_starts(device)
            return 0, (found[0] // (heads - 2) if part == 0 else found[part - 3])

        return pl.BlockSpec((rows, widths[part]), place)

    out = jax.ShapeDtypeStruct((group // 2, rows, 2 * heads * HD), jnp.bfloat16)
    return pl.pallas_call(
        functools.partial(heads_copy_kernel, members=group, parts=3),
        grid_spec=pltpu.PrefetchScalarGridSpec(
            num_scalar_prefetch=1,
            grid=(2,),
            in_specs=[spec(s, part) for s in range(group) for part in range(3)],
            out_specs=[pl.BlockSpec((group // 2, rows, heads * HD), lambda i, at: (0, 0, i))] * 2,
        ),
        out_shape=[out] * 2,
        cost_estimate=SMALL,
        name="pack_heads",
    )(lax.axis_index("mp")[None].astype(jnp.int32), *[weight] * (3 * group))


class Order:
    def __init__(self):
        self.last = None

    def tie(self, *values):
        if self.last is None:
            return values
        return lax.optimization_barrier((*values, self.last))[:-1]

    def settle(self, *values):
        *values, self.last = lax.optimization_barrier((*values, self.last))
        return values


class Job:
    def __init__(self, order, width, finish):
        self.order, self.width, self.finish = order, width, finish
        self.bits = bits_of(lax.axis_size("dp"))
        self.waiting = [None, None]
        self.columns = slice(None)

    def send_weights(self):
        near, far = (array[:, :, self.columns] for array in self.order.tie(*self.stored))
        self.near, self.far_core = [near[0]], [far[0]]
        self.packets = []
        for s in range(1, near.shape[0]):
            payload = jnp.stack([near[s], far[s]])
            self.order.last = payload
            self.packets.append(swap(payload, "mp", 2 * s))

    def join_weights(self):
        packets = self.order.tie(*self.packets)
        rows = [*self.near, *[p[0] for p in packets], *self.far_core, *[p[1] for p in packets]]
        self.weights = [
            jnp.concatenate([part[:, a * self.width : (a + 1) * self.width] for part in rows])
            for a in range(2)
        ]
        every = range(lax.axis_size("dp"))
        self.arrived = [{s: [] for s in every} for _ in range(2)]
        self.remaining = [list(every) for _ in range(2)]
        self.order.last = self.weights[0]

    def partial(self, half, which):
        blocks = self.blocks
        left = blocks[which[0]] if len(which) == 1 else jnp.concatenate([blocks[s] for s in which])
        return jnp.dot(left, self.weights[half], preferred_element_type=jnp.float32)

    def total(self, half, which, partial):
        for parts in zip(*[self.arrived[half][s] for s in which]):
            joined = parts[0] if len(which) == 1 else jnp.concatenate(parts)
            partial = partial + joined.astype(jnp.float32)
        return partial

    def product(self, half, which):
        return self.total(half, which, self.partial(half, which))

    def prepare(self, half, level):
        bit = (self.bits[::-1] if half else self.bits)[level]
        leaving = [s for s in self.remaining[half] if s & bit]
        self.remaining[half] = [s for s in self.remaining[half] if not s & bit]
        partial = self.partial(half, leaving)
        return leaving, bit, partial.astype(jnp.bfloat16) if level == 0 else partial

    def leave(self, half, prepared):
        leaving, bit, partial = prepared
        self.waiting[half] = [s ^ bit for s in leaving]
        return self.total(half, leaving, partial).astype(jnp.bfloat16)

    def land(self, half, received):
        tokens = received.shape[0] // len(self.waiting[half])
        for i, s in enumerate(self.waiting[half]):
            self.arrived[half][s].append(received[i * tokens : (i + 1) * tokens])

    def last_far(self):
        far = self.product(1, [0]).astype(jnp.bfloat16)
        self.order.last = far
        self.far = swap(far, "mp", lax.axis_size("mp") // 2)

    def close(self):
        (far,) = self.order.tie(self.far)
        self.result = self.finish(self.product(0, [0]), far)
        self.order.last = self.result


def feed_forward_jobs(order, cols, side_width):
    width = min(side_width // 2, cols) // 128 * 128
    widths = [width] * (cols // width) + ([cols % width] if cols % width else [])

    def finish_for(width):
        def finish(near, far):
            both = near + far.astype(jnp.float32)
            return (jax.nn.silu(both[:, :width]) * both[:, width:]).astype(jnp.bfloat16)

        return finish

    jobs = []
    for at, width in enumerate(widths):
        jobs.append(Job(order, 2 * width, finish_for(width)))
        jobs[-1].offset = sum(widths[:at])
    return jobs


def store_feed_forward(order, members, weight, cols):
    half_cols = weight.shape[1] // 2
    width = members[0].width // 2
    starts = []
    for job in members:
        for base in (0, half_cols):
            starts.append(lambda device, at=base + job.offset: device * cols + at)
    (weight,) = order.tie(weight)
    near, far = pack_columns(weight, starts, width)
    order.last = near
    far = swap(far, "mp", 1)
    for k, job in enumerate(members):
        job.stored, job.columns = (near, far), slice(k * 4 * width, (k + 1) * 4 * width)


def run_jobs(jobs, extras):
    order, bits = jobs[0].order, jobs[0].bits
    levels, count = len(bits), len(jobs)
    flying = []
    for turn in range(count + levels + 1):
        if 0 < turn < count:
            jobs[turn].join_weights()
        riders = []
        for level in range(levels):
            for half in (1, 0):
                if 0 <= turn - level < count:
                    job = jobs[turn - level]
                    riders.append((half, job, job.prepare(half, level)))
        landed = []
        if riders:
            partials = order.tie(*[prepared[2] for _, _, prepared in riders])
            riders = [
                (half, job, (*prepared[:2], partial))
                for (half, job, prepared), partial in zip(riders, partials)
            ]
            order.last = partials[0]
        if flying:
            landed = order.tie(*[received for received, _ in flying])
        for received, (_, members) in zip(landed, flying):
            at = 0
            for half, job, size in members:
                job.land(half, received[at : at + size])
                at += size
        flying = []
        grouped = {}
        for half, job, prepared in riders:
            part = job.leave(half, prepared)
            grouped.setdefault((prepared[1], job.width), []).append((half, job, part))
        payloads = [
            parts[0][2] if len(parts) == 1 else jnp.concatenate([part for _, _, part in parts])
            for parts in grouped.values()
        ]
        for ((bit, _), parts), payload in zip(grouped.items(), payloads):
            order.last = payload
            members = [(half, job, part.shape[0]) for half, job, part in parts]
            flying.append((swap(payload, "dp", bit), members))
        if turn + 2 < count and turn > levels:
            jobs[turn - levels - 1].close()
        if 0 <= turn - levels < count:
            jobs[turn - levels].last_far()
        if turn + 2 < count:
            jobs[turn + 2].send_weights()
        elif turn > levels:
            jobs[turn - levels - 1].close()
        for extra in extras.pop(turn, ()):
            extra()


def heads_kernel(near_ref, far_ref, cos_ref, sin_ref, q_ref, kv_ref):
    turned = (near_ref.shape[1] // HD) - 1
    for h in range(turned + 1):
        at = slice(h * HD, (h + 1) * HD)
        head = near_ref[:, at] + far_ref[:, at].astype(jnp.float32)
        if h < turned:
            head = head * cos_ref[...] + pltpu.roll(head, HD // 2, 1) * sin_ref[...]
        if h < turned - 1:
            q_ref[:, at] = head.astype(jnp.bfloat16)
        else:
            kv_ref[:, (h + 1 - turned) * HD : (h + 2 - turned) * HD] = head.astype(jnp.bfloat16)


def finish_heads(near, far, positions):
    half_dim = HD // 2
    frequency = THETA ** (-jnp.arange(half_dim, dtype=jnp.float32) / half_dim)
    angles = positions.astype(jnp.float32)[:, None] * frequency[None, :]
    cosine, sine = jnp.cos(angles), jnp.sin(angles)
    tokens, width = near.shape
    return pl.pallas_call(
        heads_kernel,
        out_shape=[
            jax.ShapeDtypeStruct((tokens, width - 2 * HD), jnp.bfloat16),
            jax.ShapeDtypeStruct((tokens, 2 * HD), jnp.bfloat16),
        ],
        cost_estimate=SMALL,
        name="finish_heads",
    )(
        near,
        far,
        jnp.concatenate([cosine, cosine], axis=1),
        jnp.concatenate([-sine, sine], axis=1),
    )


def gather_rows(at_ref, piece_refs, rows_ref):
    tokens = piece_refs[0].shape[0]
    s = 0
    for piece_ref in piece_refs:
        for i in range(piece_ref.shape[0] // tokens):
            start = pl.multiple_of((at_ref[0] ^ s) * tokens, 128)
            block = piece_ref[i * tokens : (i + 1) * tokens, :]
            rows_ref[pl.ds(start, tokens), :] = block.astype(rows_ref.dtype)
            s += 1


def attend_kernel(at_ref, q_ref, first_ref, token_ref, *refs):
    *piece_refs, out_ref, rows_ref = refs

    @pl.when(pl.program_id(0) == 0)
    def _():
        gather_rows(at_ref, piece_refs, rows_ref)

    scores = lax.dot_general(
        q_ref[...],
        rows_ref[:, :HD],
        (((1,), (1,)), ((), ())),
        preferred_element_type=jnp.float32,
    ) * HD ** (-0.5)
    key_ids = lax.broadcasted_iota(jnp.int32, scores.shape, 1)
    allowed = (key_ids >= first_ref[...]) & (key_ids <= token_ref[...])
    scores = jnp.where(allowed, scores, -jnp.inf)
    peak = jnp.max(scores, axis=-1, keepdims=True)
    weights = jnp.exp(scores - peak)
    probs = (weights / jnp.sum(weights, axis=-1, keepdims=True)).astype(jnp.bfloat16)
    attended = jnp.dot(probs, rows_ref[:, HD:], preferred_element_type=jnp.float32)
    out_ref[...] = attended.astype(jnp.bfloat16)


def attend(queries, pieces, first, token, at):
    tokens, width = queries.shape
    total = sum(piece.shape[0] for piece in pieces)
    heads = width // HD
    return pl.pallas_call(
        attend_kernel,
        grid_spec=pltpu.PrefetchScalarGridSpec(
            num_scalar_prefetch=1,
            grid=(heads,),
            in_specs=[
                pl.BlockSpec((tokens, HD), lambda h, at: (0, h)),
                pl.BlockSpec((tokens, 1), lambda h, at: (0, 0)),
                pl.BlockSpec((tokens, 1), lambda h, at: (0, 0)),
                *[pl.BlockSpec(piece.shape, lambda h, at: (0, 0)) for piece in pieces],
            ],
            out_specs=pl.BlockSpec((tokens, HD), lambda h, at: (0, h)),
            scratch_shapes=[pltpu.VMEM((total, 2 * HD), jnp.bfloat16)],
        ),
        out_shape=jax.ShapeDtypeStruct((tokens, width), jnp.bfloat16),
        cost_estimate=SMALL,
        name="attend",
    )(at, queries, first, token, *pieces)


def pages_kernel(at_ref, start_ref, count_ref, *refs):
    *piece_refs, out_ref, rows_ref = refs
    group = out_ref.shape[0]

    @pl.when(pl.program_id(0) == 0)
    def _():
        gather_rows(at_ref, piece_refs, rows_ref)
        tail = rows_ref.shape[0] - PAGE
        rows_ref[tail:, :] = jnp.zeros((PAGE, rows_ref.shape[1]), rows_ref.dtype)

    base = pl.program_id(0) * group
    for i in range(group):
        start = start_ref[base + i]
        shift = lax.rem(start, 8)
        tall = rows_ref[pl.ds(pl.multiple_of(start - shift, 8), PAGE + 8), :]
        page = pltpu.roll(tall, lax.rem(PAGE + 8 - shift, PAGE + 8), 0)[:PAGE]
        inside = lax.broadcasted_iota(jnp.int32, page.shape, 0)
        out_ref[i] = jnp.where(inside < count_ref[base + i], page, 0.0).astype(jnp.bfloat16)


def fill_pages(pieces, start, count, at):
    slots, width = start.shape[0], pieces[0].shape[1]
    total = sum(piece.shape[0] for piece in pieces)
    return pl.pallas_call(
        pages_kernel,
        grid_spec=pltpu.PrefetchScalarGridSpec(
            num_scalar_prefetch=3,
            grid=(slots // SLOT_GROUP,),
            in_specs=[pl.BlockSpec(piece.shape, lambda i, *_: (0, 0)) for piece in pieces],
            out_specs=pl.BlockSpec((SLOT_GROUP, PAGE, width), lambda i, *_: (i, 0, 0)),
            scratch_shapes=[pltpu.VMEM((total + PAGE, width), jnp.float32)],
        ),
        out_shape=jax.ShapeDtypeStruct((slots, PAGE, width), jnp.bfloat16),
        cost_estimate=SMALL,
        name="fill_pages",
    )(at, start, count, *pieces)


def page_sources(prompt_lengths, starts, request_prompt, page_table, slots):
    pages_per = page_table.shape[1]
    slot_ids = lax.axis_index("dp") * slots + jnp.arange(slots, dtype=jnp.int32)
    flat_table = page_table.reshape(-1)
    matches = slot_ids[:, None] == flat_table[None, :]
    is_used = jnp.any(matches, axis=1)
    entry_ids = jnp.sum(
        jnp.where(matches, jnp.arange(flat_table.shape[0], dtype=jnp.int32)[None, :], 0), axis=1
    )
    request_ids = entry_ids // pages_per
    offset = (entry_ids % pages_per) * PAGE
    request_match = (
        request_ids[:, None] == jnp.arange(request_prompt.shape[0], dtype=jnp.int32)[None, :]
    )
    prompt_pick = jnp.sum(jnp.where(request_match, request_prompt[None, :], 0), axis=1)
    prompt_match = (
        prompt_pick[:, None] == jnp.arange(prompt_lengths.shape[0], dtype=jnp.int32)[None, :]
    )
    slot_start = jnp.sum(jnp.where(prompt_match, starts[None, :], 0), axis=1)
    slot_length = jnp.sum(jnp.where(prompt_match, prompt_lengths[None, :], 0), axis=1)
    count = jnp.where(is_used, jnp.clip(slot_length - offset, 0, PAGE), 0)
    return jnp.where(count > 0, slot_start + offset, 0), count


def shards(
    attn_input,
    attn_gain,
    qkv_weight,
    mlp_input,
    mlp_gain,
    gate_up_weight,
    prompt_lengths,
    request_prompt,
    page_table,
):
    model_ways = lax.axis_size("mp")
    quarter_count = model_ways // KVH
    heads_here = HEADS // model_ways
    piece_dim = HD // quarter_count
    tok_here = attn_input.shape[0]
    rows = qkv_weight.shape[0]

    data_at = lax.axis_index("dp")
    at = data_at[None].astype(jnp.int32)
    token_ids = data_at * tok_here + jnp.arange(tok_here, dtype=jnp.int32)
    starts = jnp.cumsum(prompt_lengths) - prompt_lengths
    begun = token_ids[:, None] >= starts[None, :]
    first = jnp.max(jnp.where(begun, starts[None, :], 0), axis=1)

    order = Order()
    held = {}

    def heads_done(near, far):
        held["queries"], kv_local = finish_heads(near, far, token_ids - first)
        held["pieces"] = [kv_local]
        return kv_local

    def spread(bit):
        def step():
            pieces = order.tie(*held["pieces"])
            joined = pieces[0] if bit == 1 else jnp.concatenate(pieces)
            order.last = joined
            held["pieces"] = [*pieces, swap(joined, "dp", bit)]

        return step

    def attention():
        pieces = order.tie(*held["pieces"])
        held["attended"] = attend(
            held["queries"], pieces, first[:, None], token_ids[:, None], at
        )
        order.last = held["attended"]
        held["pieces"] = pieces

    def paging():
        pieces = order.tie(*held["pieces"])
        if quarter_count > 1:
            piece_at = (lax.axis_index("mp") // KVH) * piece_dim
            pieces = [
                jnp.concatenate(
                    [
                        lax.dynamic_slice_in_dim(piece, side + piece_at, piece_dim, 1)
                        for side in (0, HD)
                    ],
                    axis=1,
                )
                for piece in pieces
            ]
        sources = page_sources(prompt_lengths, starts, request_prompt, page_table, SLOT_DEV)
        held["kv_cache"] = fill_pages(pieces, *sources, at)
        order.last = held["kv_cache"]

    def head_starts(device):
        kv_head, quarter = device % KVH, device // KVH
        query = (kv_head * quarter_count + quarter) * heads_here
        return [*[query + h for h in range(heads_here)], HEADS + kv_head, HEADS + KVH + kv_head]

    model_ways_cols = gate_up_weight.shape[1] // 2 // model_ways
    heads_job = Job(order, (heads_here + 2) * HD, heads_done)
    jobs = [heads_job, *feed_forward_jobs(order, model_ways_cols, heads_job.width)]
    near, far = pack_heads(qkv_weight, head_starts)
    order.last = near
    heads_job.stored = (near, swap(far, "mp", 1))
    tokens = Tokens(order, (attn_input, mlp_input), (attn_gain, mlp_gain), rows)
    first_jobs, last_jobs = jobs[2:], []
    while first_jobs and first_jobs[-1].width != jobs[1].width:
        last_jobs = [first_jobs.pop(), *last_jobs]
    store_feed_forward(order, jobs[1:2], gate_up_weight, model_ways_cols)
    heads_job.send_weights()
    for members in (first_jobs, last_jobs):
        if members:
            store_feed_forward(order, members, gate_up_weight, model_ways_cols)
    jobs[1].send_weights()
    heads_job.join_weights()
    for members in (first_jobs, last_jobs):
        if members:
            stored = order.settle(*members[0].stored)
            for job in members:
                job.stored = stored
    heads_job.blocks, mlp_blocks = tokens.blocks()
    for job in jobs[1:]:
        job.blocks = mlp_blocks

    levels = len(heads_job.bits)
    final = len(jobs) + levels
    late = [*[spread(bit) for bit in heads_job.bits], attention, paging]
    extras = {}
    for i, extra in enumerate(late):
        turn = max(levels + 1, final - 2 - levels + min(i, levels))
        extras.setdefault(min(turn, final), []).append(extra)
    run_jobs(jobs, extras)
    hidden = jnp.concatenate([job.result for job in jobs[1:]], axis=1)
    return (held["attended"], hidden, held["kv_cache"])


def solution(mesh):
    data_ways = mesh.shape["dp"]
    placed = (
        P("dp", None),
        P(),
        P(("dp", "mp"), None),
        P("dp", None),
        P(),
        P(("dp", "mp"), None),
        P(),
        P(),
        P(),
    )

    def run(*args):
        return jax.shard_map(
            shards,
            mesh=mesh,
            in_specs=placed,
            out_specs=(P("dp", "mp"), P("dp", "mp"), P("dp", None, "mp")),
            check_vma=False,
        )(*args)

    return run
```

```python
import functools

import jax
import jax.numpy as jnp
from jax import lax
from jax.experimental import pallas as pl
from jax.experimental.pallas import tpu as pltpu
from jax.sharding import PartitionSpec as P

HEADS = 32
KVH = 8
HD = 128
PAGE = 128
EPS = 1e-05
THETA = 100000000.0
SLOT_DEV = 96
SLOT_GROUP = 8
SMALL = pl.CostEstimate(flops=1, transcendentals=0, bytes_accessed=1)


def rms_norm(stream, gain_row):
    widened = stream.astype(jnp.float32)
    squares = jnp.mean(widened * widened, axis=-1, keepdims=True)
    return (widened * lax.rsqrt(squares + EPS) * gain_row).astype(jnp.bfloat16)


def swap(value, axis, offset):
    ways = lax.axis_size(axis)
    return lax.ppermute(value, axis, [(i, i ^ offset) for i in range(ways)])


def bits_of(ways):
    return [1 << i for i in range(ways.bit_length() - 1)]


def member_order(group):
    return [*range(0, group, 2), *range(1, group, 2)]


def token_cells(streams, gains, rows):
    data_ways = lax.axis_size("dp")
    group = lax.axis_size("mp") // 2
    data_at, model_at = lax.axis_index("dp"), lax.axis_index("mp")
    cells = []
    for stream, gain_row in zip(streams, gains):
        tokens = stream.shape[0]
        half = lax.dynamic_index_in_dim(
            rms_norm(stream, gain_row).reshape(tokens, data_ways, 2, group, rows),
            model_at // group,
            2,
            keepdims=False,
        )
        members = jnp.array(member_order(group), dtype=jnp.int32) ^ (model_at % group)
        half = jnp.take(half, members, axis=2).transpose(1, 0, 2, 3)
        cells.append(half.reshape(data_ways, tokens, group * rows))
    own = [lax.dynamic_index_in_dim(cell, data_at, 0, keepdims=False) for cell in cells]
    both = jnp.concatenate(cells, axis=1)
    away = [
        lax.dynamic_index_in_dim(both, data_at ^ s, 0, keepdims=False) for s in range(1, data_ways)
    ]
    return [*own, *away]


def token_kernel(at_ref, *refs, group, rows, streams):
    data_at, side, member = at_ref[0], at_ref[1], at_ref[2]
    width = group * rows
    own_refs = refs[2 * streams : 3 * streams]
    away_refs = refs[3 * streams :]
    for k in range(streams):
        stream_ref, gain_ref = refs[k], refs[streams + k]
        tokens = stream_ref.shape[0]
        widened = stream_ref[...].astype(jnp.float32)
        scale = lax.rsqrt(jnp.mean(widened * widened, axis=-1, keepdims=True) + EPS)
        for s in range(len(away_refs) + 1):
            start = pl.multiple_of(((data_at ^ s) * 2 + side) * width, 128)
            block = stream_ref[:, pl.ds(start, width)].astype(jnp.float32)
            block = block * scale * gain_ref[:, pl.ds(start, width)]
            pieces = [block[:, i * rows : (i + 1) * rows] for i in range(group)]
            for bit in bits_of(group):
                pieces = [
                    jnp.where((member & bit) != 0, pieces[i ^ bit], pieces[i]) for i in range(group)
                ]
            block = jnp.concatenate([pieces[i] for i in member_order(group)], axis=1)
            block = block.astype(jnp.bfloat16)
            if s == 0:
                own_refs[k][...] = block
            else:
                away_refs[s - 1][k * tokens : (k + 1) * tokens, :] = block


def token_cells_kernel(streams, gains, rows):
    data_ways = lax.axis_size("dp")
    group = lax.axis_size("mp") // 2
    tokens, depth = streams[0].shape
    count = len(streams)
    model_at = lax.axis_index("mp")
    at = jnp.stack([lax.axis_index("dp"), model_at // group, model_at % group]).astype(jnp.int32)
    outs = [(tokens, group * rows)] * count
    outs += [(count * tokens, group * rows)] * (data_ways - 1)
    return pl.pallas_call(
        functools.partial(token_kernel, group=group, rows=rows, streams=count),
        grid_spec=pltpu.PrefetchScalarGridSpec(
            num_scalar_prefetch=1,
            grid=(1,),
            in_specs=[pl.BlockSpec((tokens, depth), lambda i, at: (0, 0))] * count
            + [pl.BlockSpec((1, depth), lambda i, at: (0, 0))] * count,
            out_specs=[pl.BlockSpec(shape, lambda i, at: (0, 0)) for shape in outs],
        ),
        out_shape=[jax.ShapeDtypeStruct(shape, jnp.bfloat16) for shape in outs],
        cost_estimate=SMALL,
        name="token_cells",
    )(at, *streams, *[gain_row[None] for gain_row in gains])


class Tokens:
    def __init__(self, order, streams, gains, rows):
        aligned = (lax.axis_size("mp") // 2 * rows) % 128 == 0
        streams = order.tie(*streams)
        cells = (token_cells_kernel if aligned else token_cells)(streams, gains, rows)
        self.order, self.own = order, cells[: len(streams)]
        order.done(self.own[0])
        self.away = [swap(cell, "dp", s + 1) for s, cell in enumerate(cells[len(streams) :])]

    def blocks(self):
        away = self.order.tie(*self.away)
        tokens = self.own[0].shape[0]
        return [
            [own, *[block[k * tokens : (k + 1) * tokens] for block in away]]
            for k, own in enumerate(self.own)
        ]


def copy_kernel(at_ref, *refs, members):
    for s in range(members):
        refs[members + s % 2][s // 2] = refs[s][...].astype(jnp.bfloat16)


def pack_columns(weight, starts, width):
    group = lax.axis_size("mp") // 2
    rows = weight.shape[0]
    count = len(starts)

    def spec(s):
        def place(i, at):
            device = ((at[0] // group) ^ (i % (2 * parts) // parts)) * group + ((at[0] % group) ^ s)
            column = starts[0](device)
            which = i // (2 * parts) * parts + i % parts
            for k in range(1, count):
                column = jnp.where(which == k, starts[k](device), column)
            return 0, pl.multiple_of(column, 128)

        return pl.BlockSpec((pl.Element(rows), pl.Element(width)), place)

    parts = 2 if count % 2 == 0 else 1
    steps = 2 * count
    out = jax.ShapeDtypeStruct((group // 2, rows, steps * width), jnp.bfloat16)
    return pl.pallas_call(
        functools.partial(copy_kernel, members=group),
        grid_spec=pltpu.PrefetchScalarGridSpec(
            num_scalar_prefetch=1,
            grid=(steps,),
            in_specs=[spec(s) for s in range(group)],
            out_specs=[pl.BlockSpec((group // 2, rows, width), lambda i, at: (0, 0, i))] * 2,
        ),
        out_shape=[out] * 2,
        cost_estimate=SMALL,
        name="pack_columns",
    )(lax.axis_index("mp")[None].astype(jnp.int32), *[weight] * group)


def heads_copy_kernel(at_ref, *refs, members, parts):
    for s in range(members):
        done = 0
        for p in range(parts):
            block = refs[s * parts + p][...].astype(jnp.bfloat16)
            refs[members * parts + s % 2][s // 2, :, done : done + block.shape[1]] = block
            done += block.shape[1]


def pack_heads(weight, head_starts):
    group = lax.axis_size("mp") // 2
    rows = weight.shape[0]
    heads = len(head_starts(0))
    widths = [(heads - 2) * HD, HD, HD]

    def spec(s, part):
        def place(i, at):
            device = ((at[0] // group) ^ i) * group + ((at[0] % group) ^ s)
            found = head_starts(device)
            return 0, (found[0] // (heads - 2) if part == 0 else found[part - 3])

        return pl.BlockSpec((rows, widths[part]), place)

    out = jax.ShapeDtypeStruct((group // 2, rows, 2 * heads * HD), jnp.bfloat16)
    return pl.pallas_call(
        functools.partial(heads_copy_kernel, members=group, parts=3),
        grid_spec=pltpu.PrefetchScalarGridSpec(
            num_scalar_prefetch=1,
            grid=(2,),
            in_specs=[spec(s, part) for s in range(group) for part in range(3)],
            out_specs=[pl.BlockSpec((group // 2, rows, heads * HD), lambda i, at: (0, 0, i))] * 2,
        ),
        out_shape=[out] * 2,
        cost_estimate=SMALL,
        name="pack_heads",
    )(lax.axis_index("mp")[None].astype(jnp.int32), *[weight] * (3 * group))


class Order:
    def __init__(self):
        self.last = []

    def done(self, *values):
        self.last = list(values)

    def tie(self, *values):
        return lax.optimization_barrier((*values, *self.last))[: len(values)]


class Job:
    def __init__(self, order, width, finish):
        self.order, self.width, self.finish = order, width, finish
        self.bits = bits_of(lax.axis_size("dp"))
        self.waiting = [None, None]
        self.columns = slice(None)
        self.stored = None

    def send_weights(self):
        near, far = (array[:, :, self.columns] for array in self.order.tie(*self.stored))
        self.near, self.far_core = [near[0]], [far[0]]
        self.packets = []
        for s in range(1, near.shape[0]):
            payload = jnp.stack([near[s], far[s]])
            self.order.done(payload)
            self.packets.append(swap(payload, "mp", 2 * s))

    def join_weights(self, others=()):
        stored = [array for job in others for array in job.stored]
        ready = self.order.tie(*self.packets, *stored)
        packets, stored = ready[: len(self.packets)], ready[len(self.packets) :]
        for i, job in enumerate(others):
            job.stored = stored[2 * i : 2 * i + 2]
        rows = [*self.near, *[p[0] for p in packets], *self.far_core, *[p[1] for p in packets]]
        self.weights = [
            jnp.concatenate([part[:, a * self.width : (a + 1) * self.width] for part in rows])
            for a in range(2)
        ]
        every = range(lax.axis_size("dp"))
        self.arrived = [{s: [] for s in every} for _ in range(2)]
        self.remaining = [list(every) for _ in range(2)]
        self.order.done(self.weights[0])

    def partial(self, half, which):
        blocks = self.blocks
        left = blocks[which[0]] if len(which) == 1 else jnp.concatenate([blocks[s] for s in which])
        return jnp.dot(left, self.weights[half], preferred_element_type=jnp.float32)

    def total(self, half, which, partial):
        for parts in zip(*[self.arrived[half][s] for s in which]):
            joined = parts[0] if len(which) == 1 else jnp.concatenate(parts)
            partial = partial + joined.astype(jnp.float32)
        return partial

    def product(self, half, which):
        return self.total(half, which, self.partial(half, which))

    def prepare(self, half, level):
        bit = (self.bits[::-1] if half else self.bits)[level]
        leaving = [s for s in self.remaining[half] if s & bit]
        self.remaining[half] = [s for s in self.remaining[half] if not s & bit]
        partial = self.partial(half, leaving)
        return leaving, bit, partial.astype(jnp.bfloat16) if level == 0 else partial

    def leave(self, half, prepared):
        leaving, bit, partial = prepared
        self.waiting[half] = [s ^ bit for s in leaving]
        return self.total(half, leaving, partial).astype(jnp.bfloat16)

    def land(self, half, received):
        tokens = received.shape[0] // len(self.waiting[half])
        for i, s in enumerate(self.waiting[half]):
            self.arrived[half][s].append(received[i * tokens : (i + 1) * tokens])

    def last_far(self):
        (partial,) = self.order.tie(self.partial(1, [0]))
        far = self.total(1, [0], partial).astype(jnp.bfloat16)
        self.order.done(far)
        self.far = swap(far, "mp", lax.axis_size("mp") // 2)

    def close(self):
        far, partial = self.order.tie(self.far, self.partial(0, [0]))
        self.result = self.finish(self.total(0, [0], partial), far)
        self.order.done(self.result)


def feed_forward_jobs(order, cols, side_width):
    width = min(side_width // 2, cols) // 128 * 128
    widths = [width] * (cols // width) + ([cols % width] if cols % width else [])

    def finish_for(width):
        def finish(near, far):
            both = near + far.astype(jnp.float32)
            return (jax.nn.silu(both[:, :width]) * both[:, width:]).astype(jnp.bfloat16)

        return finish

    jobs = []
    for at, width in enumerate(widths):
        jobs.append(Job(order, 2 * width, finish_for(width)))
        jobs[-1].offset = sum(widths[:at])
    return jobs


def store_feed_forward(order, members, weight, cols):
    half_cols = weight.shape[1] // 2
    width = members[0].width // 2
    starts = []
    for job in members:
        for base in (0, half_cols):
            starts.append(lambda device, at=base + job.offset: device * cols + at)
    (weight,) = order.tie(weight)
    near, far = pack_columns(weight, starts, width)
    order.done(near)
    far = swap(far, "mp", 1)
    for k, job in enumerate(members):
        job.stored, job.columns = (near, far), slice(k * 4 * width, (k + 1) * 4 * width)


def run_jobs(jobs, last_jobs, store_last, early, late):
    order, bits = jobs[0].order, jobs[0].bits
    levels, count = len(bits), len(jobs)
    flying = []
    for turn in range(count + levels + 1):
        if 0 < turn < count:
            jobs[turn].join_weights(last_jobs[:1] if turn == 1 else ())
            for job in last_jobs[1:] if turn == 1 else ():
                job.stored = last_jobs[0].stored
        for extra in early.get(turn, ()):
            extra()
        riders = []
        for level in range(levels):
            for half in (1, 0):
                if 0 <= turn - level < count:
                    job = jobs[turn - level]
                    riders.append((half, job, job.prepare(half, level)))
        ready = order.tie(
            *[received for received, _ in flying], *[prepared[2] for _, _, prepared in riders]
        )
        landed, partials = ready[: len(flying)], ready[len(flying) :]
        riders = [
            (half, job, (*prepared[:2], partial))
            for (half, job, prepared), partial in zip(riders, partials)
        ]
        for received, (_, members) in zip(landed, flying):
            at = 0
            for half, job, size in members:
                job.land(half, received[at : at + size])
                at += size
        flying = []
        grouped = {}
        for half, job, prepared in riders:
            part = job.leave(half, prepared)
            grouped.setdefault((prepared[1], job.width), []).append((half, job, part))
        payloads = [
            parts[0][2] if len(parts) == 1 else jnp.concatenate([part for _, _, part in parts])
            for parts in grouped.values()
        ]
        if payloads:
            order.done(*payloads)
        for ((bit, _), parts), payload in zip(grouped.items(), payloads):
            members = [(half, job, part.shape[0]) for half, job, part in parts]
            flying.append((swap(payload, "dp", bit), members))
        if turn + 2 < count and turn > levels:
            jobs[turn - levels - 1].close()
        if 0 <= turn - levels < count:
            jobs[turn - levels].last_far()
        if turn + 2 < count:
            jobs[turn + 2].send_weights()
        elif turn > levels:
            jobs[turn - levels - 1].close()
        if turn == 0:
            store_last()
        for extra in late.get(turn, ()):
            extra()


def heads_kernel(near_ref, far_ref, cos_ref, sin_ref, q_ref, kv_ref):
    turned = (near_ref.shape[1] // HD) - 1
    for h in range(turned + 1):
        at = slice(h * HD, (h + 1) * HD)
        head = near_ref[:, at] + far_ref[:, at].astype(jnp.float32)
        if h < turned:
            head = head * cos_ref[...] + pltpu.roll(head, HD // 2, 1) * sin_ref[...]
        if h < turned - 1:
            q_ref[:, at] = head.astype(jnp.bfloat16)
        else:
            kv_ref[:, (h + 1 - turned) * HD : (h + 2 - turned) * HD] = head.astype(jnp.bfloat16)


def finish_heads(near, far, positions):
    half_dim = HD // 2
    frequency = THETA ** (-jnp.arange(half_dim, dtype=jnp.float32) / half_dim)
    angles = positions.astype(jnp.float32)[:, None] * frequency[None, :]
    cosine, sine = jnp.cos(angles), jnp.sin(angles)
    tokens, width = near.shape
    return pl.pallas_call(
        heads_kernel,
        out_shape=[
            jax.ShapeDtypeStruct((tokens, width - 2 * HD), jnp.bfloat16),
            jax.ShapeDtypeStruct((tokens, 2 * HD), jnp.bfloat16),
        ],
        cost_estimate=SMALL,
        name="finish_heads",
    )(
        near,
        far,
        jnp.concatenate([cosine, cosine], axis=1),
        jnp.concatenate([-sine, sine], axis=1),
    )


def gather_rows(at_ref, piece_refs, rows_ref):
    tokens = piece_refs[0].shape[0]
    s = 0
    for piece_ref in piece_refs:
        for i in range(piece_ref.shape[0] // tokens):
            start = pl.multiple_of((at_ref[0] ^ s) * tokens, 128)
            block = piece_ref[i * tokens : (i + 1) * tokens, :]
            rows_ref[pl.ds(start, tokens), :] = block.astype(rows_ref.dtype)
            s += 1


def attend_kernel(at_ref, q_ref, first_ref, token_ref, *refs):
    *piece_refs, out_ref, rows_ref = refs

    @pl.when(pl.program_id(0) == 0)
    def _():
        gather_rows(at_ref, piece_refs, rows_ref)

    scores = lax.dot_general(
        q_ref[...],
        rows_ref[:, :HD],
        (((1,), (1,)), ((), ())),
        preferred_element_type=jnp.float32,
    ) * HD ** (-0.5)
    key_ids = lax.broadcasted_iota(jnp.int32, scores.shape, 1)
    allowed = (key_ids >= first_ref[...]) & (key_ids <= token_ref[...])
    scores = jnp.where(allowed, scores, -jnp.inf)
    peak = jnp.max(scores, axis=-1, keepdims=True)
    weights = jnp.exp(scores - peak)
    probs = (weights / jnp.sum(weights, axis=-1, keepdims=True)).astype(jnp.bfloat16)
    attended = jnp.dot(probs, rows_ref[:, HD:], preferred_element_type=jnp.float32)
    out_ref[...] = attended.astype(jnp.bfloat16)


def attend(queries, pieces, first, token, at):
    tokens, width = queries.shape
    total = sum(piece.shape[0] for piece in pieces)
    heads = width // HD
    return pl.pallas_call(
        attend_kernel,
        grid_spec=pltpu.PrefetchScalarGridSpec(
            num_scalar_prefetch=1,
            grid=(heads,),
            in_specs=[
                pl.BlockSpec((tokens, HD), lambda h, at: (0, h)),
                pl.BlockSpec((tokens, 1), lambda h, at: (0, 0)),
                pl.BlockSpec((tokens, 1), lambda h, at: (0, 0)),
                *[pl.BlockSpec(piece.shape, lambda h, at: (0, 0)) for piece in pieces],
            ],
            out_specs=pl.BlockSpec((tokens, HD), lambda h, at: (0, h)),
            scratch_shapes=[pltpu.VMEM((total, 2 * HD), jnp.bfloat16)],
        ),
        out_shape=jax.ShapeDtypeStruct((tokens, width), jnp.bfloat16),
        cost_estimate=SMALL,
        name="attend",
    )(at, queries, first, token, *pieces)


def pages_kernel(at_ref, start_ref, count_ref, *refs):
    *piece_refs, out_ref, rows_ref = refs
    group = out_ref.shape[0]

    @pl.when(pl.program_id(0) == 0)
    def _():
        gather_rows(at_ref, piece_refs, rows_ref)
        tail = rows_ref.shape[0] - PAGE
        rows_ref[tail:, :] = jnp.zeros((PAGE, rows_ref.shape[1]), rows_ref.dtype)

    base = pl.program_id(0) * group
    for i in range(group):
        start = start_ref[base + i]
        shift = lax.rem(start, 8)
        tall = rows_ref[pl.ds(pl.multiple_of(start - shift, 8), PAGE + 8), :]
        page = pltpu.roll(tall, lax.rem(PAGE + 8 - shift, PAGE + 8), 0)[:PAGE]
        inside = lax.broadcasted_iota(jnp.int32, page.shape, 0)
        out_ref[i] = jnp.where(inside < count_ref[base + i], page, 0.0).astype(jnp.bfloat16)


def fill_pages(pieces, start, count, at):
    slots, width = start.shape[0], pieces[0].shape[1]
    total = sum(piece.shape[0] for piece in pieces)
    return pl.pallas_call(
        pages_kernel,
        grid_spec=pltpu.PrefetchScalarGridSpec(
            num_scalar_prefetch=3,
            grid=(slots // SLOT_GROUP,),
            in_specs=[pl.BlockSpec(piece.shape, lambda i, *_: (0, 0)) for piece in pieces],
            out_specs=pl.BlockSpec((SLOT_GROUP, PAGE, width), lambda i, *_: (i, 0, 0)),
            scratch_shapes=[pltpu.VMEM((total + PAGE, width), jnp.float32)],
        ),
        out_shape=jax.ShapeDtypeStruct((slots, PAGE, width), jnp.bfloat16),
        cost_estimate=SMALL,
        name="fill_pages",
    )(at, start, count, *pieces)


def page_sources(prompt_lengths, starts, request_prompt, page_table, slots):
    pages_per = page_table.shape[1]
    slot_ids = lax.axis_index("dp") * slots + jnp.arange(slots, dtype=jnp.int32)
    flat_table = page_table.reshape(-1)
    matches = slot_ids[:, None] == flat_table[None, :]
    is_used = jnp.any(matches, axis=1)
    entry_ids = jnp.sum(
        jnp.where(matches, jnp.arange(flat_table.shape[0], dtype=jnp.int32)[None, :], 0), axis=1
    )
    request_ids = entry_ids // pages_per
    offset = (entry_ids % pages_per) * PAGE
    request_match = (
        request_ids[:, None] == jnp.arange(request_prompt.shape[0], dtype=jnp.int32)[None, :]
    )
    prompt_pick = jnp.sum(jnp.where(request_match, request_prompt[None, :], 0), axis=1)
    prompt_match = (
        prompt_pick[:, None] == jnp.arange(prompt_lengths.shape[0], dtype=jnp.int32)[None, :]
    )
    slot_start = jnp.sum(jnp.where(prompt_match, starts[None, :], 0), axis=1)
    slot_length = jnp.sum(jnp.where(prompt_match, prompt_lengths[None, :], 0), axis=1)
    count = jnp.where(is_used, jnp.clip(slot_length - offset, 0, PAGE), 0)
    return jnp.where(count > 0, slot_start + offset, 0), count


def shards(
    attn_input,
    attn_gain,
    qkv_weight,
    mlp_input,
    mlp_gain,
    gate_up_weight,
    prompt_lengths,
    request_prompt,
    page_table,
):
    model_ways = lax.axis_size("mp")
    quarter_count = model_ways // KVH
    heads_here = HEADS // model_ways
    piece_dim = HD // quarter_count
    tok_here = attn_input.shape[0]
    rows = qkv_weight.shape[0]

    data_at = lax.axis_index("dp")
    at = data_at[None].astype(jnp.int32)
    token_ids = data_at * tok_here + jnp.arange(tok_here, dtype=jnp.int32)
    starts = jnp.cumsum(prompt_lengths) - prompt_lengths
    begun = token_ids[:, None] >= starts[None, :]
    first = jnp.max(jnp.where(begun, starts[None, :], 0), axis=1)

    order = Order()
    held = {}

    def heads_done(near, far):
        held["queries"], kv_local = finish_heads(near, far, token_ids - first)
        held["pieces"] = [kv_local]
        return kv_local

    def spread(bit):
        def step():
            pieces = order.tie(*held["pieces"])
            joined = pieces[0] if bit == 1 else jnp.concatenate(pieces)
            order.done(joined)
            held["pieces"] = [*pieces, swap(joined, "dp", bit)]

        return step

    def attention():
        pieces = order.tie(*held["pieces"])
        held["attended"] = attend(
            held["queries"], pieces, first[:, None], token_ids[:, None], at
        )
        order.done(held["attended"])
        held["pieces"] = pieces

    def paging():
        pieces = order.tie(*held["pieces"])
        if quarter_count > 1:
            piece_at = (lax.axis_index("mp") // KVH) * piece_dim
            pieces = [
                jnp.concatenate(
                    [
                        lax.dynamic_slice_in_dim(piece, side + piece_at, piece_dim, 1)
                        for side in (0, HD)
                    ],
                    axis=1,
                )
                for piece in pieces
            ]
        sources = page_sources(prompt_lengths, starts, request_prompt, page_table, SLOT_DEV)
        held["kv_cache"] = fill_pages(pieces, *sources, at)
        order.done(held["kv_cache"])

    def head_starts(device):
        kv_head, quarter = device % KVH, device // KVH
        query = (kv_head * quarter_count + quarter) * heads_here
        return [*[query + h for h in range(heads_here)], HEADS + kv_head, HEADS + KVH + kv_head]

    model_ways_cols = gate_up_weight.shape[1] // 2 // model_ways
    heads_job = Job(order, (heads_here + 2) * HD, heads_done)
    jobs = [heads_job, *feed_forward_jobs(order, model_ways_cols, heads_job.width)]
    near, far = pack_heads(qkv_weight, head_starts)
    order.done(near)
    heads_job.stored = (near, swap(far, "mp", 1))
    first_jobs, last_jobs = jobs[2:], []
    while first_jobs and first_jobs[-1].width != jobs[1].width:
        last_jobs = [first_jobs.pop(), *last_jobs]
    store_feed_forward(order, jobs[1:2], gate_up_weight, model_ways_cols)
    tokens = Tokens(order, (attn_input, mlp_input), (attn_gain, mlp_gain), rows)
    heads_job.send_weights()
    jobs[1].send_weights()
    if first_jobs:
        store_feed_forward(order, first_jobs, gate_up_weight, model_ways_cols)
    heads_job.join_weights()
    heads_job.blocks, mlp_blocks = tokens.blocks()
    for job in jobs[1:]:
        job.blocks = mlp_blocks

    def store_last():
        if last_jobs:
            store_feed_forward(order, last_jobs, gate_up_weight, model_ways_cols)

    levels = len(heads_job.bits)
    final = len(jobs) + levels
    early = {}
    for i, bit in enumerate(heads_job.bits):
        early.setdefault(min(levels + 2 + i, final), []).append(spread(bit))
    late = {min(2 * levels + 1, final): [attention, paging]}
    run_jobs(jobs, last_jobs, store_last, early, late)
    hidden = jnp.concatenate([job.result for job in jobs[1:]], axis=1)
    return (held["attended"], hidden, held["kv_cache"])


def solution(mesh):
    data_ways = mesh.shape["dp"]
    placed = (
        P("dp", None),
        P(),
        P(("dp", "mp"), None),
        P("dp", None),
        P(),
        P(("dp", "mp"), None),
        P(),
        P(),
        P(),
    )

    def run(*args):
        return jax.shard_map(
            shards,
            mesh=mesh,
            in_specs=placed,
            out_specs=(P("dp", "mp"), P("dp", "mp"), P("dp", None, "mp")),
            check_vma=False,
        )(*args)

    return run
```

```python
import functools

import jax
import jax.numpy as jnp
from jax import lax
from jax.experimental import pallas as pl
from jax.experimental.pallas import tpu as pltpu
from jax.sharding import PartitionSpec as P

HEADS = 32
KVH = 8
HD = 128
PAGE = 128
EPS = 1e-05
THETA = 100000000.0
SLOT_DEV = 96
SLOT_GROUP = 8
TOKEN_ROWS = 64
SMALL = pl.CostEstimate(flops=1, transcendentals=0, bytes_accessed=1)


def rms_norm(stream, gain_row):
    widened = stream.astype(jnp.float32)
    squares = jnp.mean(widened * widened, axis=-1, keepdims=True)
    return (widened * lax.rsqrt(squares + EPS) * gain_row).astype(jnp.bfloat16)


def swap(value, axis, offset):
    ways = lax.axis_size(axis)
    return lax.ppermute(value, axis, [(i, i ^ offset) for i in range(ways)])


def bits_of(ways):
    return [1 << i for i in range(ways.bit_length() - 1)]


def member_order(group):
    return [*range(0, group, 2), *range(1, group, 2)]


def token_cells(streams, gains, rows):
    data_ways = lax.axis_size("dp")
    group = lax.axis_size("mp") // 2
    data_at, model_at = lax.axis_index("dp"), lax.axis_index("mp")
    cells = []
    for stream, gain_row in zip(streams, gains):
        tokens = stream.shape[0]
        half = lax.dynamic_index_in_dim(
            rms_norm(stream, gain_row).reshape(tokens, data_ways, 2, group, rows),
            model_at // group,
            2,
            keepdims=False,
        )
        members = jnp.array(member_order(group), dtype=jnp.int32) ^ (model_at % group)
        half = jnp.take(half, members, axis=2).transpose(1, 0, 2, 3)
        cells.append(half.reshape(data_ways, tokens, group * rows))
    own = [lax.dynamic_index_in_dim(cell, data_at, 0, keepdims=False) for cell in cells]
    both = jnp.stack(cells, axis=1)
    away = [
        lax.dynamic_index_in_dim(both, data_at ^ s, 0, keepdims=False) for s in range(1, data_ways)
    ]
    return [*own, *away]


def token_kernel(at_ref, *refs, group, rows, streams):
    data_at, side, member = at_ref[0], at_ref[1], at_ref[2]
    width = group * rows
    own_refs = refs[2 * streams : 3 * streams]
    away_refs = refs[3 * streams :]
    for k in range(streams):
        stream_ref, gain_ref = refs[k], refs[streams + k]
        widened = stream_ref[...].astype(jnp.float32)
        scale = lax.rsqrt(jnp.mean(widened * widened, axis=-1, keepdims=True) + EPS)
        for s in range(len(away_refs) + 1):
            start = pl.multiple_of(((data_at ^ s) * 2 + side) * width, 128)
            block = stream_ref[:, pl.ds(start, width)].astype(jnp.float32)
            block = (block * scale * gain_ref[:, pl.ds(start, width)]).astype(jnp.bfloat16)
            pieces = [block[:, i * rows : (i + 1) * rows] for i in range(group)]
            for bit in bits_of(group):
                pieces = [
                    jnp.where((member & bit) != 0, pieces[i ^ bit], pieces[i]) for i in range(group)
                ]
            block = jnp.concatenate([pieces[i] for i in member_order(group)], axis=1)
            if s == 0:
                own_refs[k][...] = block
            else:
                away_refs[s - 1][k] = block


def token_cells_kernel(streams, gains, rows):
    data_ways = lax.axis_size("dp")
    group = lax.axis_size("mp") // 2
    tokens, depth = streams[0].shape
    count = len(streams)
    step = TOKEN_ROWS
    model_at = lax.axis_index("mp")
    at = jnp.stack([lax.axis_index("dp"), model_at // group, model_at % group]).astype(jnp.int32)
    width = group * rows
    return pl.pallas_call(
        functools.partial(token_kernel, group=group, rows=rows, streams=count),
        grid_spec=pltpu.PrefetchScalarGridSpec(
            num_scalar_prefetch=1,
            grid=(tokens // step,),
            in_specs=[pl.BlockSpec((step, depth), lambda i, at: (i, 0))] * count
            + [pl.BlockSpec((1, depth), lambda i, at: (0, 0))] * count,
            out_specs=[pl.BlockSpec((step, width), lambda i, at: (i, 0))] * count
            + [pl.BlockSpec((count, step, width), lambda i, at: (0, i, 0))] * (data_ways - 1),
        ),
        out_shape=[jax.ShapeDtypeStruct((tokens, width), jnp.bfloat16)] * count
        + [jax.ShapeDtypeStruct((count, tokens, width), jnp.bfloat16)] * (data_ways - 1),
        cost_estimate=SMALL,
        name="token_cells",
    )(at, *streams, *[gain_row[None] for gain_row in gains])


class Tokens:
    def __init__(self, order, streams, gains, rows):
        aligned = (lax.axis_size("mp") // 2 * rows) % 128 == 0
        streams = order.tie(*streams)
        cells = (token_cells_kernel if aligned else token_cells)(streams, gains, rows)
        self.order, self.own = order, cells[: len(streams)]
        order.done(self.own[0])
        self.away = [swap(cell, "dp", s + 1) for s, cell in enumerate(cells[len(streams) :])]

    def blocks(self):
        away = self.order.tie(*self.away)
        return [[own, *[block[k] for block in away]] for k, own in enumerate(self.own)]


def copy_kernel(at_ref, *refs, members):
    for s in range(members):
        refs[members + s % 2][s // 2] = refs[s][...].astype(jnp.bfloat16)


def pack_columns(weight, starts, width):
    group = lax.axis_size("mp") // 2
    rows = weight.shape[0]
    count = len(starts)

    def spec(s):
        def place(i, at):
            device = ((at[0] // group) ^ (i % (2 * parts) // parts)) * group + ((at[0] % group) ^ s)
            column = starts[0](device)
            which = i // (2 * parts) * parts + i % parts
            for k in range(1, count):
                column = jnp.where(which == k, starts[k](device), column)
            return 0, pl.multiple_of(column, 128)

        return pl.BlockSpec((pl.Element(rows), pl.Element(width)), place)

    parts = 2 if count % 2 == 0 else 1
    steps = 2 * count
    out = jax.ShapeDtypeStruct((group // 2, rows, steps * width), jnp.bfloat16)
    return pl.pallas_call(
        functools.partial(copy_kernel, members=group),
        grid_spec=pltpu.PrefetchScalarGridSpec(
            num_scalar_prefetch=1,
            grid=(steps,),
            in_specs=[spec(s) for s in range(group)],
            out_specs=[pl.BlockSpec((group // 2, rows, width), lambda i, at: (0, 0, i))] * 2,
        ),
        out_shape=[out] * 2,
        cost_estimate=SMALL,
        name="pack_columns",
    )(lax.axis_index("mp")[None].astype(jnp.int32), *[weight] * group)


def heads_copy_kernel(at_ref, *refs, members, parts):
    for s in range(members):
        done = 0
        for p in range(parts):
            block = refs[s * parts + p][...].astype(jnp.bfloat16)
            refs[members * parts + s % 2][s // 2, :, done : done + block.shape[1]] = block
            done += block.shape[1]


def pack_heads(weight, head_starts):
    group = lax.axis_size("mp") // 2
    rows = weight.shape[0]
    heads = len(head_starts(0))
    widths = [(heads - 2) * HD, HD, HD]

    def spec(s, part):
        def place(i, at):
            device = ((at[0] // group) ^ i) * group + ((at[0] % group) ^ s)
            found = head_starts(device)
            return 0, (found[0] // (heads - 2) if part == 0 else found[part - 3])

        return pl.BlockSpec((rows, widths[part]), place)

    out = jax.ShapeDtypeStruct((group // 2, rows, 2 * heads * HD), jnp.bfloat16)
    return pl.pallas_call(
        functools.partial(heads_copy_kernel, members=group, parts=3),
        grid_spec=pltpu.PrefetchScalarGridSpec(
            num_scalar_prefetch=1,
            grid=(2,),
            in_specs=[spec(s, part) for s in range(group) for part in range(3)],
            out_specs=[pl.BlockSpec((group // 2, rows, heads * HD), lambda i, at: (0, 0, i))] * 2,
        ),
        out_shape=[out] * 2,
        cost_estimate=SMALL,
        name="pack_heads",
    )(lax.axis_index("mp")[None].astype(jnp.int32), *[weight] * (3 * group))


class Order:
    def __init__(self):
        self.last = []

    def done(self, *values):
        self.last = list(values)

    def tie(self, *values):
        return lax.optimization_barrier((*values, *self.last))[: len(values)]


class Job:
    def __init__(self, order, width, finish):
        self.order, self.width, self.finish = order, width, finish
        self.bits = bits_of(lax.axis_size("dp"))
        self.waiting = [None, None]
        self.columns = slice(None)
        self.stored = None

    def send_weights(self):
        near, far = (array[:, :, self.columns] for array in self.order.tie(*self.stored))
        self.near, self.far_core = [near[0]], [far[0]]
        self.packets = []
        for s in range(1, near.shape[0]):
            payload = jnp.stack([near[s], far[s]])
            self.order.done(payload)
            self.packets.append(swap(payload, "mp", 2 * s))

    def join_weights(self, others=()):
        stored = [array for job in others for array in job.stored]
        ready = self.order.tie(*self.packets, *stored)
        packets, stored = ready[: len(self.packets)], ready[len(self.packets) :]
        for i, job in enumerate(others):
            job.stored = stored[2 * i : 2 * i + 2]
        rows = [*self.near, *[p[0] for p in packets], *self.far_core, *[p[1] for p in packets]]
        self.weights = [
            jnp.concatenate([part[:, a * self.width : (a + 1) * self.width] for part in rows])
            for a in range(2)
        ]
        every = range(lax.axis_size("dp"))
        self.arrived = [{s: [] for s in every} for _ in range(2)]
        self.remaining = [list(every) for _ in range(2)]
        self.order.done(self.weights[0])

    def partial(self, half, which):
        blocks = self.blocks
        left = blocks[which[0]] if len(which) == 1 else jnp.concatenate([blocks[s] for s in which])
        return jnp.dot(left, self.weights[half], preferred_element_type=jnp.float32)

    def total(self, half, which, partial):
        for parts in zip(*[self.arrived[half][s] for s in which]):
            joined = parts[0] if len(which) == 1 else jnp.concatenate(parts)
            partial = partial + joined.astype(jnp.float32)
        return partial

    def product(self, half, which):
        return self.total(half, which, self.partial(half, which))

    def prepare(self, half, level):
        bit = (self.bits[::-1] if half else self.bits)[level]
        leaving = [s for s in self.remaining[half] if s & bit]
        self.remaining[half] = [s for s in self.remaining[half] if not s & bit]
        partial = self.partial(half, leaving)
        return leaving, bit, partial.astype(jnp.bfloat16) if level == 0 else partial

    def leave(self, half, prepared):
        leaving, bit, partial = prepared
        self.waiting[half] = [s ^ bit for s in leaving]
        return self.total(half, leaving, partial).astype(jnp.bfloat16)

    def land(self, half, received):
        tokens = received.shape[0] // len(self.waiting[half])
        for i, s in enumerate(self.waiting[half]):
            self.arrived[half][s].append(received[i * tokens : (i + 1) * tokens])

    def last_far(self):
        (partial,) = self.order.tie(self.partial(1, [0]))
        far = self.total(1, [0], partial).astype(jnp.bfloat16)
        self.order.done(far)
        self.far = swap(far, "mp", lax.axis_size("mp") // 2)

    def close(self):
        far, partial = self.order.tie(self.far, self.partial(0, [0]))
        self.result = self.finish(self.total(0, [0], partial), far)
        self.order.done(self.result)


def feed_forward_jobs(order, cols, side_width):
    width = min(side_width // 2, cols) // 128 * 128
    widths = [width] * (cols // width) + ([cols % width] if cols % width else [])

    def finish_for(width):
        def finish(near, far):
            both = near + far.astype(jnp.float32)
            return (jax.nn.silu(both[:, :width]) * both[:, width:]).astype(jnp.bfloat16)

        return finish

    jobs = []
    for at, width in enumerate(widths):
        jobs.append(Job(order, 2 * width, finish_for(width)))
        jobs[-1].offset = sum(widths[:at])
    return jobs


def store_feed_forward(order, members, weight, cols):
    half_cols = weight.shape[1] // 2
    width = members[0].width // 2
    starts = []
    for job in members:
        for base in (0, half_cols):
            starts.append(lambda device, at=base + job.offset: device * cols + at)
    (weight,) = order.tie(weight)
    near, far = pack_columns(weight, starts, width)
    order.done(near)
    far = swap(far, "mp", 1)
    for k, job in enumerate(members):
        job.stored, job.columns = (near, far), slice(k * 4 * width, (k + 1) * 4 * width)


def run_jobs(jobs, last_jobs, store_last, early, late):
    order, bits = jobs[0].order, jobs[0].bits
    levels, count = len(bits), len(jobs)
    flying = []
    for turn in range(count + levels + 1):
        if 0 < turn < count:
            jobs[turn].join_weights(last_jobs[:1] if turn == 1 else ())
            for job in last_jobs[1:] if turn == 1 else ():
                job.stored = last_jobs[0].stored
        for extra in early.get(turn, ()):
            extra()
        riders = []
        for level in range(levels):
            for half in (1, 0):
                if 0 <= turn - level < count:
                    job = jobs[turn - level]
                    riders.append((half, job, job.prepare(half, level)))
        ready = order.tie(
            *[received for received, _ in flying], *[prepared[2] for _, _, prepared in riders]
        )
        landed, partials = ready[: len(flying)], ready[len(flying) :]
        riders = [
            (half, job, (*prepared[:2], partial))
            for (half, job, prepared), partial in zip(riders, partials)
        ]
        for received, (_, members) in zip(landed, flying):
            at = 0
            for half, job, size in members:
                job.land(half, received[at : at + size])
                at += size
        flying = []
        grouped = {}
        for half, job, prepared in riders:
            part = job.leave(half, prepared)
            grouped.setdefault((prepared[1], job.width), []).append((half, job, part))
        payloads = [
            parts[0][2] if len(parts) == 1 else jnp.concatenate([part for _, _, part in parts])
            for parts in grouped.values()
        ]
        if payloads:
            order.done(*payloads)
        for ((bit, _), parts), payload in zip(grouped.items(), payloads):
            members = [(half, job, part.shape[0]) for half, job, part in parts]
            flying.append((swap(payload, "dp", bit), members))
        if turn + 2 < count and turn > levels:
            jobs[turn - levels - 1].close()
        if 0 <= turn - levels < count:
            jobs[turn - levels].last_far()
        if turn + 2 < count:
            jobs[turn + 2].send_weights()
        elif turn > levels:
            jobs[turn - levels - 1].close()
        if turn == 0:
            store_last()
        for extra in late.get(turn, ()):
            extra()


def heads_kernel(near_ref, far_ref, cos_ref, sin_ref, q_ref, kv_ref):
    turned = (near_ref.shape[1] // HD) - 1
    for h in range(turned + 1):
        at = slice(h * HD, (h + 1) * HD)
        head = near_ref[:, at] + far_ref[:, at].astype(jnp.float32)
        if h < turned:
            head = head * cos_ref[...] + pltpu.roll(head, HD // 2, 1) * sin_ref[...]
        if h < turned - 1:
            q_ref[:, at] = head.astype(jnp.bfloat16)
        else:
            kv_ref[:, (h + 1 - turned) * HD : (h + 2 - turned) * HD] = head.astype(jnp.bfloat16)


def finish_heads(near, far, positions):
    half_dim = HD // 2
    frequency = THETA ** (-jnp.arange(half_dim, dtype=jnp.float32) / half_dim)
    angles = positions.astype(jnp.float32)[:, None] * frequency[None, :]
    cosine, sine = jnp.cos(angles), jnp.sin(angles)
    tokens, width = near.shape
    return pl.pallas_call(
        heads_kernel,
        out_shape=[
            jax.ShapeDtypeStruct((tokens, width - 2 * HD), jnp.bfloat16),
            jax.ShapeDtypeStruct((tokens, 2 * HD), jnp.bfloat16),
        ],
        cost_estimate=SMALL,
        name="finish_heads",
    )(
        near,
        far,
        jnp.concatenate([cosine, cosine], axis=1),
        jnp.concatenate([-sine, sine], axis=1),
    )


def gather_rows(at_ref, piece_refs, rows_ref):
    tokens = piece_refs[0].shape[0]
    s = 0
    for piece_ref in piece_refs:
        for i in range(piece_ref.shape[0] // tokens):
            start = pl.multiple_of((at_ref[0] ^ s) * tokens, 128)
            block = piece_ref[i * tokens : (i + 1) * tokens, :]
            rows_ref[pl.ds(start, tokens), :] = block.astype(rows_ref.dtype)
            s += 1


def attend_kernel(at_ref, q_ref, first_ref, token_ref, *refs):
    *piece_refs, out_ref, rows_ref = refs

    @pl.when(pl.program_id(0) == 0)
    def _():
        gather_rows(at_ref, piece_refs, rows_ref)

    scores = lax.dot_general(
        q_ref[...],
        rows_ref[:, :HD],
        (((1,), (1,)), ((), ())),
        preferred_element_type=jnp.float32,
    ) * HD ** (-0.5)
    key_ids = lax.broadcasted_iota(jnp.int32, scores.shape, 1)
    allowed = (key_ids >= first_ref[...]) & (key_ids <= token_ref[...])
    scores = jnp.where(allowed, scores, -jnp.inf)
    peak = jnp.max(scores, axis=-1, keepdims=True)
    weights = jnp.exp(scores - peak)
    probs = (weights / jnp.sum(weights, axis=-1, keepdims=True)).astype(jnp.bfloat16)
    attended = jnp.dot(probs, rows_ref[:, HD:], preferred_element_type=jnp.float32)
    out_ref[...] = attended.astype(jnp.bfloat16)


def attend(queries, pieces, first, token, at):
    tokens, width = queries.shape
    total = sum(piece.shape[0] for piece in pieces)
    heads = width // HD
    return pl.pallas_call(
        attend_kernel,
        grid_spec=pltpu.PrefetchScalarGridSpec(
            num_scalar_prefetch=1,
            grid=(heads,),
            in_specs=[
                pl.BlockSpec((tokens, HD), lambda h, at: (0, h)),
                pl.BlockSpec((tokens, 1), lambda h, at: (0, 0)),
                pl.BlockSpec((tokens, 1), lambda h, at: (0, 0)),
                *[pl.BlockSpec(piece.shape, lambda h, at: (0, 0)) for piece in pieces],
            ],
            out_specs=pl.BlockSpec((tokens, HD), lambda h, at: (0, h)),
            scratch_shapes=[pltpu.VMEM((total, 2 * HD), jnp.bfloat16)],
        ),
        out_shape=jax.ShapeDtypeStruct((tokens, width), jnp.bfloat16),
        cost_estimate=SMALL,
        name="attend",
    )(at, queries, first, token, *pieces)


def pages_kernel(at_ref, start_ref, count_ref, *refs):
    *piece_refs, out_ref, rows_ref = refs
    group = out_ref.shape[0]

    @pl.when(pl.program_id(0) == 0)
    def _():
        gather_rows(at_ref, piece_refs, rows_ref)
        tail = rows_ref.shape[0] - PAGE
        rows_ref[tail:, :] = jnp.zeros((PAGE, rows_ref.shape[1]), rows_ref.dtype)

    base = pl.program_id(0) * group

    def fill(i, carry):
        start = start_ref[base + i]
        shift = lax.rem(start, 8)
        tall = rows_ref[pl.ds(pl.multiple_of(start - shift, 8), PAGE + 8), :]
        page = pltpu.roll(tall, lax.rem(PAGE + 8 - shift, PAGE + 8), 0)[:PAGE]
        inside = lax.broadcasted_iota(jnp.int32, page.shape, 0)
        out_ref[i] = jnp.where(inside < count_ref[base + i], page, 0.0).astype(jnp.bfloat16)
        return carry

    lax.fori_loop(0, group, fill, 0)


def fill_pages(pieces, start, count, at):
    slots, width = start.shape[0], pieces[0].shape[1]
    total = sum(piece.shape[0] for piece in pieces)
    return pl.pallas_call(
        pages_kernel,
        grid_spec=pltpu.PrefetchScalarGridSpec(
            num_scalar_prefetch=3,
            grid=(slots // SLOT_GROUP,),
            in_specs=[pl.BlockSpec(piece.shape, lambda i, *_: (0, 0)) for piece in pieces],
            out_specs=pl.BlockSpec((SLOT_GROUP, PAGE, width), lambda i, *_: (i, 0, 0)),
            scratch_shapes=[pltpu.VMEM((total + PAGE, width), jnp.float32)],
        ),
        out_shape=jax.ShapeDtypeStruct((slots, PAGE, width), jnp.bfloat16),
        cost_estimate=SMALL,
        name="fill_pages",
    )(at, start, count, *pieces)


def page_sources(prompt_lengths, starts, request_prompt, page_table, slots):
    pages_per = page_table.shape[1]
    slot_ids = lax.axis_index("dp") * slots + jnp.arange(slots, dtype=jnp.int32)
    flat_table = page_table.reshape(-1)
    matches = slot_ids[:, None] == flat_table[None, :]
    is_used = jnp.any(matches, axis=1)
    entry_ids = jnp.sum(
        jnp.where(matches, jnp.arange(flat_table.shape[0], dtype=jnp.int32)[None, :], 0), axis=1
    )
    request_ids = entry_ids // pages_per
    offset = (entry_ids % pages_per) * PAGE
    request_match = (
        request_ids[:, None] == jnp.arange(request_prompt.shape[0], dtype=jnp.int32)[None, :]
    )
    prompt_pick = jnp.sum(jnp.where(request_match, request_prompt[None, :], 0), axis=1)
    prompt_match = (
        prompt_pick[:, None] == jnp.arange(prompt_lengths.shape[0], dtype=jnp.int32)[None, :]
    )
    slot_start = jnp.sum(jnp.where(prompt_match, starts[None, :], 0), axis=1)
    slot_length = jnp.sum(jnp.where(prompt_match, prompt_lengths[None, :], 0), axis=1)
    count = jnp.where(is_used, jnp.clip(slot_length - offset, 0, PAGE), 0)
    return jnp.where(count > 0, slot_start + offset, 0), count


def shards(
    attn_input,
    attn_gain,
    qkv_weight,
    mlp_input,
    mlp_gain,
    gate_up_weight,
    prompt_lengths,
    request_prompt,
    page_table,
):
    model_ways = lax.axis_size("mp")
    quarter_count = model_ways // KVH
    heads_here = HEADS // model_ways
    piece_dim = HD // quarter_count
    tok_here = attn_input.shape[0]
    rows = qkv_weight.shape[0]

    data_at = lax.axis_index("dp")
    at = data_at[None].astype(jnp.int32)
    token_ids = data_at * tok_here + jnp.arange(tok_here, dtype=jnp.int32)
    starts = jnp.cumsum(prompt_lengths) - prompt_lengths
    begun = token_ids[:, None] >= starts[None, :]
    first = jnp.max(jnp.where(begun, starts[None, :], 0), axis=1)

    order = Order()
    held = {}

    def heads_done(near, far):
        held["queries"], kv_local = finish_heads(near, far, token_ids - first)
        held["pieces"] = [kv_local]
        return kv_local

    def spread(bit):
        def step():
            pieces = order.tie(*held["pieces"])
            joined = pieces[0] if bit == 1 else jnp.concatenate(pieces)
            order.done(joined)
            held["pieces"] = [*pieces, swap(joined, "dp", bit)]

        return step

    def attention():
        pieces = order.tie(*held["pieces"])
        held["attended"] = attend(
            held["queries"], pieces, first[:, None], token_ids[:, None], at
        )
        order.done(held["attended"])
        held["pieces"] = pieces

    def paging():
        pieces = order.tie(*held["pieces"])
        if quarter_count > 1:
            piece_at = (lax.axis_index("mp") // KVH) * piece_dim
            pieces = [
                jnp.concatenate(
                    [
                        lax.dynamic_slice_in_dim(piece, side + piece_at, piece_dim, 1)
                        for side in (0, HD)
                    ],
                    axis=1,
                )
                for piece in pieces
            ]
        sources = page_sources(prompt_lengths, starts, request_prompt, page_table, SLOT_DEV)
        held["kv_cache"] = fill_pages(pieces, *sources, at)
        order.done(held["kv_cache"])

    def head_starts(device):
        kv_head, quarter = device % KVH, device // KVH
        query = (kv_head * quarter_count + quarter) * heads_here
        return [*[query + h for h in range(heads_here)], HEADS + kv_head, HEADS + KVH + kv_head]

    model_ways_cols = gate_up_weight.shape[1] // 2 // model_ways
    heads_job = Job(order, (heads_here + 2) * HD, heads_done)
    jobs = [heads_job, *feed_forward_jobs(order, model_ways_cols, heads_job.width)]
    near, far = pack_heads(qkv_weight, head_starts)
    order.done(near)
    heads_job.stored = (near, swap(far, "mp", 1))
    first_jobs, last_jobs = jobs[2:], []
    while first_jobs and first_jobs[-1].width != jobs[1].width:
        last_jobs = [first_jobs.pop(), *last_jobs]
    store_feed_forward(order, jobs[1:2], gate_up_weight, model_ways_cols)
    tokens = Tokens(order, (attn_input, mlp_input), (attn_gain, mlp_gain), rows)
    heads_job.send_weights()
    jobs[1].send_weights()
    if first_jobs:
        store_feed_forward(order, first_jobs, gate_up_weight, model_ways_cols)
    heads_job.join_weights()
    heads_job.blocks, mlp_blocks = tokens.blocks()
    for job in jobs[1:]:
        job.blocks = mlp_blocks

    def store_last():
        if last_jobs:
            store_feed_forward(order, last_jobs, gate_up_weight, model_ways_cols)

    levels = len(heads_job.bits)
    final = len(jobs) + levels
    early = {}
    for i, bit in enumerate(heads_job.bits):
        early.setdefault(min(levels + 2 + i, final), []).append(spread(bit))
    late = {min(2 * levels + 1, final): [attention, paging]}
    run_jobs(jobs, last_jobs, store_last, early, late)
    hidden = jnp.concatenate([job.result for job in jobs[1:]], axis=1)
    return (held["attended"], hidden, held["kv_cache"])


def solution(mesh):
    data_ways = mesh.shape["dp"]
    placed = (
        P("dp", None),
        P(),
        P(("dp", "mp"), None),
        P("dp", None),
        P(),
        P(("dp", "mp"), None),
        P(),
        P(),
        P(),
    )

    def run(*args):
        return jax.shard_map(
            shards,
            mesh=mesh,
            in_specs=placed,
            out_specs=(P("dp", "mp"), P("dp", "mp"), P("dp", None, "mp")),
            check_vma=False,
        )(*args)

    return run
```

```python
import functools

import jax
import jax.numpy as jnp
from jax import lax
from jax.experimental import pallas as pl
from jax.experimental.pallas import tpu as pltpu
from jax.sharding import PartitionSpec as P

HEADS = 32
KVH = 8
HD = 128
PAGE = 128
EPS = 1e-05
THETA = 100000000.0
SLOT_DEV = 96
SLOT_GROUP = 8
TOKEN_ROWS = 64
SMALL = pl.CostEstimate(flops=1, transcendentals=0, bytes_accessed=1)


def rms_norm(stream, gain_row):
    widened = stream.astype(jnp.float32)
    squares = jnp.mean(widened * widened, axis=-1, keepdims=True)
    return (widened * lax.rsqrt(squares + EPS) * gain_row).astype(jnp.bfloat16)


def swap(value, axis, offset):
    ways = lax.axis_size(axis)
    return lax.ppermute(value, axis, [(i, i ^ offset) for i in range(ways)])


def bits_of(ways):
    return [1 << i for i in range(ways.bit_length() - 1)]


def member_order(group):
    return [*range(0, group, 2), *range(1, group, 2)]


def token_cells(streams, gains, rows):
    data_ways = lax.axis_size("dp")
    group = lax.axis_size("mp") // 2
    data_at, model_at = lax.axis_index("dp"), lax.axis_index("mp")
    cells = []
    for stream, gain_row in zip(streams, gains):
        tokens = stream.shape[0]
        half = lax.dynamic_index_in_dim(
            rms_norm(stream, gain_row).reshape(tokens, data_ways, 2, group, rows),
            model_at // group,
            2,
            keepdims=False,
        )
        members = jnp.array(member_order(group), dtype=jnp.int32) ^ (model_at % group)
        half = jnp.take(half, members, axis=2).transpose(1, 0, 2, 3)
        cells.append(half.reshape(data_ways, tokens, group * rows))
    own = [lax.dynamic_index_in_dim(cell, data_at, 0, keepdims=False) for cell in cells]
    both = jnp.stack(cells, axis=1)
    away = [
        lax.dynamic_index_in_dim(both, data_at ^ s, 0, keepdims=False) for s in range(1, data_ways)
    ]
    return [*own, *away]


def token_kernel(at_ref, *refs, group, rows, streams):
    data_at, side, member = at_ref[0], at_ref[1], at_ref[2]
    width = group * rows
    own_refs = refs[2 * streams : 3 * streams]
    away_refs = refs[3 * streams :]
    for k in range(streams):
        stream_ref, gain_ref = refs[k], refs[streams + k]
        widened = stream_ref[...].astype(jnp.float32)
        scale = lax.rsqrt(jnp.mean(widened * widened, axis=-1, keepdims=True) + EPS)
        for s in range(len(away_refs) + 1):
            start = pl.multiple_of(((data_at ^ s) * 2 + side) * width, 128)
            block = stream_ref[:, pl.ds(start, width)].astype(jnp.float32)
            block = (block * scale * gain_ref[:, pl.ds(start, width)]).astype(jnp.bfloat16)
            pieces = [block[:, i * rows : (i + 1) * rows] for i in range(group)]
            for bit in bits_of(group):
                pieces = [
                    jnp.where((member & bit) != 0, pieces[i ^ bit], pieces[i]) for i in range(group)
                ]
            block = jnp.concatenate([pieces[i] for i in member_order(group)], axis=1)
            if s == 0:
                own_refs[k][...] = block
            else:
                away_refs[s - 1][k] = block


def token_cells_kernel(streams, gains, rows):
    data_ways = lax.axis_size("dp")
    group = lax.axis_size("mp") // 2
    tokens, depth = streams[0].shape
    count = len(streams)
    step = TOKEN_ROWS
    model_at = lax.axis_index("mp")
    at = jnp.stack([lax.axis_index("dp"), model_at // group, model_at % group]).astype(jnp.int32)
    width = group * rows
    return pl.pallas_call(
        functools.partial(token_kernel, group=group, rows=rows, streams=count),
        grid_spec=pltpu.PrefetchScalarGridSpec(
            num_scalar_prefetch=1,
            grid=(tokens // step,),
            in_specs=[pl.BlockSpec((step, depth), lambda i, at: (i, 0))] * count
            + [pl.BlockSpec((1, depth), lambda i, at: (0, 0))] * count,
            out_specs=[pl.BlockSpec((step, width), lambda i, at: (i, 0))] * count
            + [pl.BlockSpec((count, step, width), lambda i, at: (0, i, 0))] * (data_ways - 1),
        ),
        out_shape=[jax.ShapeDtypeStruct((tokens, width), jnp.bfloat16)] * count
        + [jax.ShapeDtypeStruct((count, tokens, width), jnp.bfloat16)] * (data_ways - 1),
        cost_estimate=SMALL,
        name="token_cells",
    )(at, *streams, *[gain_row[None] for gain_row in gains])


class Tokens:
    def __init__(self, order, streams, gains, rows):
        aligned = (lax.axis_size("mp") // 2 * rows) % 128 == 0
        streams = order.tie(*streams)
        cells = (token_cells_kernel if aligned else token_cells)(streams, gains, rows)
        self.order, self.own = order, cells[: len(streams)]
        order.done(self.own[0])
        self.away = [swap(cell, "dp", s + 1) for s, cell in enumerate(cells[len(streams) :])]

    def blocks(self):
        away = self.order.tie(*self.away)
        return [[own, *[block[k] for block in away]] for k, own in enumerate(self.own)]


def copy_kernel(at_ref, *refs, members):
    for s in range(members):
        refs[members + s % 2][s // 2] = refs[s][...].astype(jnp.bfloat16)


def pack_columns(weight, starts, width):
    group = lax.axis_size("mp") // 2
    rows = weight.shape[0]
    count = len(starts)

    def spec(s):
        def place(i, at):
            device = ((at[0] // group) ^ (i % (2 * parts) // parts)) * group + ((at[0] % group) ^ s)
            column = starts[0](device)
            which = i // (2 * parts) * parts + i % parts
            for k in range(1, count):
                column = jnp.where(which == k, starts[k](device), column)
            return 0, pl.multiple_of(column, 128)

        return pl.BlockSpec((pl.Element(rows), pl.Element(width)), place)

    parts = 2 if count % 2 == 0 else 1
    steps = 2 * count
    out = jax.ShapeDtypeStruct((group // 2, rows, steps * width), jnp.bfloat16)
    return pl.pallas_call(
        functools.partial(copy_kernel, members=group),
        grid_spec=pltpu.PrefetchScalarGridSpec(
            num_scalar_prefetch=1,
            grid=(steps,),
            in_specs=[spec(s) for s in range(group)],
            out_specs=[pl.BlockSpec((group // 2, rows, width), lambda i, at: (0, 0, i))] * 2,
        ),
        out_shape=[out] * 2,
        cost_estimate=SMALL,
        name="pack_columns",
    )(lax.axis_index("mp")[None].astype(jnp.int32), *[weight] * group)


def heads_copy_kernel(at_ref, *refs, members, parts):
    for s in range(members):
        done = 0
        for p in range(parts):
            block = refs[s * parts + p][...].astype(jnp.bfloat16)
            refs[members * parts + s % 2][s // 2, :, done : done + block.shape[1]] = block
            done += block.shape[1]


def pack_heads(weight, head_starts):
    group = lax.axis_size("mp") // 2
    rows = weight.shape[0]
    heads = len(head_starts(0))
    widths = [(heads - 2) * HD, HD, HD]

    def spec(s, part):
        def place(i, at):
            device = ((at[0] // group) ^ i) * group + ((at[0] % group) ^ s)
            found = head_starts(device)
            return 0, (found[0] // (heads - 2) if part == 0 else found[part - 3])

        return pl.BlockSpec((rows, widths[part]), place)

    out = jax.ShapeDtypeStruct((group // 2, rows, 2 * heads * HD), jnp.bfloat16)
    return pl.pallas_call(
        functools.partial(heads_copy_kernel, members=group, parts=3),
        grid_spec=pltpu.PrefetchScalarGridSpec(
            num_scalar_prefetch=1,
            grid=(2,),
            in_specs=[spec(s, part) for s in range(group) for part in range(3)],
            out_specs=[pl.BlockSpec((group // 2, rows, heads * HD), lambda i, at: (0, 0, i))] * 2,
        ),
        out_shape=[out] * 2,
        cost_estimate=SMALL,
        name="pack_heads",
    )(lax.axis_index("mp")[None].astype(jnp.int32), *[weight] * (3 * group))


class Order:
    def __init__(self):
        self.last = []

    def done(self, *values):
        self.last = list(values)

    def tie(self, *values):
        return lax.optimization_barrier((*values, *self.last))[: len(values)]


class Job:
    def __init__(self, order, width, finish):
        self.order, self.width, self.finish = order, width, finish
        self.bits = bits_of(lax.axis_size("dp"))
        self.waiting = [None, None]
        self.columns = slice(None)
        self.stored = None

    def send_weights(self):
        near, far = (array[:, :, self.columns] for array in self.order.tie(*self.stored))
        self.near, self.far_core = [near[0]], [far[0]]
        self.packets = []
        for s in range(1, near.shape[0]):
            payload = jnp.stack([near[s], far[s]])
            self.order.done(payload)
            self.packets.append(swap(payload, "mp", 2 * s))

    def join_weights(self, others=()):
        stored = [array for job in others for array in job.stored]
        ready = self.order.tie(*self.packets, *stored)
        packets, stored = ready[: len(self.packets)], ready[len(self.packets) :]
        for i, job in enumerate(others):
            job.stored = stored[2 * i : 2 * i + 2]
        rows = [*self.near, *[p[0] for p in packets], *self.far_core, *[p[1] for p in packets]]
        self.weights = [
            jnp.concatenate([part[:, a * self.width : (a + 1) * self.width] for part in rows])
            for a in range(2)
        ]
        every = range(lax.axis_size("dp"))
        self.arrived = [{s: [] for s in every} for _ in range(2)]
        self.remaining = [list(every) for _ in range(2)]
        self.order.done(self.weights[0])

    def partial(self, half, which):
        blocks = self.blocks
        left = blocks[which[0]] if len(which) == 1 else jnp.concatenate([blocks[s] for s in which])
        return jnp.dot(left, self.weights[half], preferred_element_type=jnp.float32)

    def total(self, half, which, partial):
        for parts in zip(*[self.arrived[half][s] for s in which]):
            joined = parts[0] if len(which) == 1 else jnp.concatenate(parts)
            partial = partial + joined.astype(jnp.float32)
        return partial

    def product(self, half, which):
        return self.total(half, which, self.partial(half, which))

    def prepare(self, half, level):
        bit = (self.bits[::-1] if half else self.bits)[level]
        leaving = [s for s in self.remaining[half] if s & bit]
        self.remaining[half] = [s for s in self.remaining[half] if not s & bit]
        partial = self.partial(half, leaving)
        return leaving, bit, partial.astype(jnp.bfloat16) if level == 0 else partial

    def leave(self, half, prepared):
        leaving, bit, partial = prepared
        self.waiting[half] = [s ^ bit for s in leaving]
        return self.total(half, leaving, partial).astype(jnp.bfloat16)

    def land(self, half, received):
        tokens = received.shape[0] // len(self.waiting[half])
        for i, s in enumerate(self.waiting[half]):
            self.arrived[half][s].append(received[i * tokens : (i + 1) * tokens])

    def last_far(self):
        (partial,) = self.order.tie(self.partial(1, [0]))
        far = self.total(1, [0], partial).astype(jnp.bfloat16)
        self.order.done(far)
        self.far = swap(far, "mp", lax.axis_size("mp") // 2)

    def close(self):
        far, partial = self.order.tie(self.far, self.partial(0, [0]))
        self.result = self.finish(self.total(0, [0], partial), far)
        self.order.done(self.result)


def feed_forward_jobs(order, cols, side_width):
    width = min(side_width // 2, cols) // 128 * 128
    widths = [width] * (cols // width) + ([cols % width] if cols % width else [])

    def finish_for(width):
        def finish(near, far):
            both = near + far.astype(jnp.float32)
            return (jax.nn.silu(both[:, :width]) * both[:, width:]).astype(jnp.bfloat16)

        return finish

    jobs = []
    for at, width in enumerate(widths):
        jobs.append(Job(order, 2 * width, finish_for(width)))
        jobs[-1].offset = sum(widths[:at])
    return jobs


def store_feed_forward(order, members, weight, cols):
    half_cols = weight.shape[1] // 2
    width = members[0].width // 2
    starts = []
    for job in members:
        for base in (0, half_cols):
            starts.append(lambda device, at=base + job.offset: device * cols + at)
    (weight,) = order.tie(weight)
    near, far = pack_columns(weight, starts, width)
    order.done(near)
    far = swap(far, "mp", 1)
    for k, job in enumerate(members):
        job.stored, job.columns = (near, far), slice(k * 4 * width, (k + 1) * 4 * width)


def run_jobs(jobs, last_jobs, store_last, early, late):
    order, bits = jobs[0].order, jobs[0].bits
    levels, count = len(bits), len(jobs)
    flying = []
    for turn in range(count + levels + 1):
        if 0 < turn < count:
            jobs[turn].join_weights(last_jobs[:1] if turn == 1 else ())
            for job in last_jobs[1:] if turn == 1 else ():
                job.stored = last_jobs[0].stored
        for extra in early.get(turn, ()):
            extra()
        riders = []
        for level in range(levels):
            for half in (1, 0):
                if 0 <= turn - level < count:
                    job = jobs[turn - level]
                    riders.append((half, job, job.prepare(half, level)))
        ready = order.tie(
            *[received for received, _ in flying], *[prepared[2] for _, _, prepared in riders]
        )
        landed, partials = ready[: len(flying)], ready[len(flying) :]
        riders = [
            (half, job, (*prepared[:2], partial))
            for (half, job, prepared), partial in zip(riders, partials)
        ]
        for received, (_, members) in zip(landed, flying):
            at = 0
            for half, job, size in members:
                job.land(half, received[at : at + size])
                at += size
        flying = []
        grouped = {}
        for half, job, prepared in riders:
            part = job.leave(half, prepared)
            grouped.setdefault((prepared[1], job.width), []).append((half, job, part))
        payloads = [
            parts[0][2] if len(parts) == 1 else jnp.concatenate([part for _, _, part in parts])
            for parts in grouped.values()
        ]
        if payloads:
            order.done(*payloads)
        for ((bit, _), parts), payload in zip(grouped.items(), payloads):
            members = [(half, job, part.shape[0]) for half, job, part in parts]
            flying.append((swap(payload, "dp", bit), members))
        if turn + 2 < count and turn > levels:
            jobs[turn - levels - 1].close()
        if 0 <= turn - levels < count:
            jobs[turn - levels].last_far()
        if turn + 2 < count:
            jobs[turn + 2].send_weights()
        if turn == 0:
            store_last()
        for extra in late.get(turn, ()):
            extra()
        if turn + 2 >= count and turn > levels:
            jobs[turn - levels - 1].close()


def heads_kernel(near_ref, far_ref, cos_ref, sin_ref, q_ref, kv_ref):
    turned = (near_ref.shape[1] // HD) - 1
    for h in range(turned + 1):
        at = slice(h * HD, (h + 1) * HD)
        head = near_ref[:, at] + far_ref[:, at].astype(jnp.float32)
        if h < turned:
            head = head * cos_ref[...] + pltpu.roll(head, HD // 2, 1) * sin_ref[...]
        if h < turned - 1:
            q_ref[:, at] = head.astype(jnp.bfloat16)
        else:
            kv_ref[:, (h + 1 - turned) * HD : (h + 2 - turned) * HD] = head.astype(jnp.bfloat16)


def finish_heads(near, far, positions):
    half_dim = HD // 2
    frequency = THETA ** (-jnp.arange(half_dim, dtype=jnp.float32) / half_dim)
    angles = positions.astype(jnp.float32)[:, None] * frequency[None, :]
    cosine, sine = jnp.cos(angles), jnp.sin(angles)
    tokens, width = near.shape
    return pl.pallas_call(
        heads_kernel,
        out_shape=[
            jax.ShapeDtypeStruct((tokens, width - 2 * HD), jnp.bfloat16),
            jax.ShapeDtypeStruct((tokens, 2 * HD), jnp.bfloat16),
        ],
        cost_estimate=SMALL,
        name="finish_heads",
    )(
        near,
        far,
        jnp.concatenate([cosine, cosine], axis=1),
        jnp.concatenate([-sine, sine], axis=1),
    )


def gather_rows(at_ref, piece_refs, rows_ref):
    tokens = piece_refs[0].shape[0]
    s = 0
    for piece_ref in piece_refs:
        for i in range(piece_ref.shape[0] // tokens):
            start = pl.multiple_of((at_ref[0] ^ s) * tokens, 128)
            block = piece_ref[i * tokens : (i + 1) * tokens, :]
            rows_ref[pl.ds(start, tokens), :] = block.astype(rows_ref.dtype)
            s += 1


def attend_kernel(at_ref, q_ref, first_ref, token_ref, *refs):
    *piece_refs, out_ref, rows_ref = refs

    @pl.when(pl.program_id(0) == 0)
    def _():
        gather_rows(at_ref, piece_refs, rows_ref)

    scores = lax.dot_general(
        q_ref[...],
        rows_ref[:, :HD],
        (((1,), (1,)), ((), ())),
        preferred_element_type=jnp.float32,
    ) * HD ** (-0.5)
    key_ids = lax.broadcasted_iota(jnp.int32, scores.shape, 1)
    allowed = (key_ids >= first_ref[...]) & (key_ids <= token_ref[...])
    scores = jnp.where(allowed, scores, -jnp.inf)
    peak = jnp.max(scores, axis=-1, keepdims=True)
    weights = jnp.exp(scores - peak)
    probs = (weights / jnp.sum(weights, axis=-1, keepdims=True)).astype(jnp.bfloat16)
    attended = jnp.dot(probs, rows_ref[:, HD:], preferred_element_type=jnp.float32)
    out_ref[...] = attended.astype(jnp.bfloat16)


def attend(queries, pieces, first, token, at):
    tokens, width = queries.shape
    total = sum(piece.shape[0] for piece in pieces)
    heads = width // HD
    return pl.pallas_call(
        attend_kernel,
        grid_spec=pltpu.PrefetchScalarGridSpec(
            num_scalar_prefetch=1,
            grid=(heads,),
            in_specs=[
                pl.BlockSpec((tokens, HD), lambda h, at: (0, h)),
                pl.BlockSpec((tokens, 1), lambda h, at: (0, 0)),
                pl.BlockSpec((tokens, 1), lambda h, at: (0, 0)),
                *[pl.BlockSpec(piece.shape, lambda h, at: (0, 0)) for piece in pieces],
            ],
            out_specs=pl.BlockSpec((tokens, HD), lambda h, at: (0, h)),
            scratch_shapes=[pltpu.VMEM((total, 2 * HD), jnp.bfloat16)],
        ),
        out_shape=jax.ShapeDtypeStruct((tokens, width), jnp.bfloat16),
        cost_estimate=SMALL,
        name="attend",
    )(at, queries, first, token, *pieces)


def pages_kernel(at_ref, start_ref, count_ref, *refs):
    *piece_refs, out_ref, rows_ref = refs
    group = out_ref.shape[0]

    @pl.when(pl.program_id(0) == 0)
    def _():
        gather_rows(at_ref, piece_refs, rows_ref)
        tail = rows_ref.shape[0] - PAGE
        rows_ref[tail:, :] = jnp.zeros((PAGE, rows_ref.shape[1]), rows_ref.dtype)

    base = pl.program_id(0) * group

    def fill(i, carry):
        start = start_ref[base + i]
        shift = lax.rem(start, 8)
        tall = rows_ref[pl.ds(pl.multiple_of(start - shift, 8), PAGE + 8), :]
        page = pltpu.roll(tall, lax.rem(PAGE + 8 - shift, PAGE + 8), 0)[:PAGE]
        inside = lax.broadcasted_iota(jnp.int32, page.shape, 0)
        out_ref[i] = jnp.where(inside < count_ref[base + i], page, 0.0).astype(jnp.bfloat16)
        return carry

    lax.fori_loop(0, group, fill, 0)


def fill_pages(pieces, start, count, at):
    slots, width = start.shape[0], pieces[0].shape[1]
    total = sum(piece.shape[0] for piece in pieces)
    return pl.pallas_call(
        pages_kernel,
        grid_spec=pltpu.PrefetchScalarGridSpec(
            num_scalar_prefetch=3,
            grid=(slots // SLOT_GROUP,),
            in_specs=[pl.BlockSpec(piece.shape, lambda i, *_: (0, 0)) for piece in pieces],
            out_specs=pl.BlockSpec((SLOT_GROUP, PAGE, width), lambda i, *_: (i, 0, 0)),
            scratch_shapes=[pltpu.VMEM((total + PAGE, width), jnp.float32)],
        ),
        out_shape=jax.ShapeDtypeStruct((slots, PAGE, width), jnp.bfloat16),
        cost_estimate=SMALL,
        name="fill_pages",
    )(at, start, count, *pieces)


def page_sources(prompt_lengths, starts, request_prompt, page_table, slots):
    pages_per = page_table.shape[1]
    slot_ids = lax.axis_index("dp") * slots + jnp.arange(slots, dtype=jnp.int32)
    flat_table = page_table.reshape(-1)
    matches = slot_ids[:, None] == flat_table[None, :]
    is_used = jnp.any(matches, axis=1)
    entry_ids = jnp.sum(
        jnp.where(matches, jnp.arange(flat_table.shape[0], dtype=jnp.int32)[None, :], 0), axis=1
    )
    request_ids = entry_ids // pages_per
    offset = (entry_ids % pages_per) * PAGE
    request_match = (
        request_ids[:, None] == jnp.arange(request_prompt.shape[0], dtype=jnp.int32)[None, :]
    )
    prompt_pick = jnp.sum(jnp.where(request_match, request_prompt[None, :], 0), axis=1)
    prompt_match = (
        prompt_pick[:, None] == jnp.arange(prompt_lengths.shape[0], dtype=jnp.int32)[None, :]
    )
    slot_start = jnp.sum(jnp.where(prompt_match, starts[None, :], 0), axis=1)
    slot_length = jnp.sum(jnp.where(prompt_match, prompt_lengths[None, :], 0), axis=1)
    count = jnp.where(is_used, jnp.clip(slot_length - offset, 0, PAGE), 0)
    return jnp.where(count > 0, slot_start + offset, 0), count


def shards(
    attn_input,
    attn_gain,
    qkv_weight,
    mlp_input,
    mlp_gain,
    gate_up_weight,
    prompt_lengths,
    request_prompt,
    page_table,
):
    model_ways = lax.axis_size("mp")
    quarter_count = model_ways // KVH
    heads_here = HEADS // model_ways
    piece_dim = HD // quarter_count
    tok_here = attn_input.shape[0]
    rows = qkv_weight.shape[0]

    data_at = lax.axis_index("dp")
    at = data_at[None].astype(jnp.int32)
    token_ids = data_at * tok_here + jnp.arange(tok_here, dtype=jnp.int32)
    starts = jnp.cumsum(prompt_lengths) - prompt_lengths
    begun = token_ids[:, None] >= starts[None, :]
    first = jnp.max(jnp.where(begun, starts[None, :], 0), axis=1)

    order = Order()
    held = {}

    def heads_done(near, far):
        held["queries"], kv_local = finish_heads(near, far, token_ids - first)
        held["pieces"] = [kv_local]
        return kv_local

    def spread(bit):
        def step():
            pieces = order.tie(*held["pieces"])
            joined = pieces[0] if bit == 1 else jnp.concatenate(pieces)
            order.done(joined)
            held["pieces"] = [*pieces, swap(joined, "dp", bit)]

        return step

    def attention():
        pieces = order.tie(*held["pieces"])
        held["attended"] = attend(
            held["queries"], pieces, first[:, None], token_ids[:, None], at
        )
        order.done(held["attended"])
        held["pieces"] = pieces

    def paging():
        pieces = order.tie(*held["pieces"])
        if quarter_count > 1:
            piece_at = (lax.axis_index("mp") // KVH) * piece_dim
            pieces = [
                jnp.concatenate(
                    [
                        lax.dynamic_slice_in_dim(piece, side + piece_at, piece_dim, 1)
                        for side in (0, HD)
                    ],
                    axis=1,
                )
                for piece in pieces
            ]
        sources = page_sources(prompt_lengths, starts, request_prompt, page_table, SLOT_DEV)
        held["kv_cache"] = fill_pages(pieces, *sources, at)
        order.done(held["kv_cache"])

    def head_starts(device):
        kv_head, quarter = device % KVH, device // KVH
        query = (kv_head * quarter_count + quarter) * heads_here
        return [*[query + h for h in range(heads_here)], HEADS + kv_head, HEADS + KVH + kv_head]

    model_ways_cols = gate_up_weight.shape[1] // 2 // model_ways
    heads_job = Job(order, (heads_here + 2) * HD, heads_done)
    jobs = [heads_job, *feed_forward_jobs(order, model_ways_cols, 1024)]
    near, far = pack_heads(qkv_weight, head_starts)
    order.done(near)
    heads_job.stored = (near, swap(far, "mp", 1))
    first_jobs, last_jobs = jobs[2:], []
    while first_jobs and first_jobs[-1].width != jobs[1].width:
        last_jobs = [first_jobs.pop(), *last_jobs]
    store_feed_forward(order, jobs[1:2], gate_up_weight, model_ways_cols)
    tokens = Tokens(order, (attn_input, mlp_input), (attn_gain, mlp_gain), rows)
    heads_job.send_weights()
    jobs[1].send_weights()
    if first_jobs:
        store_feed_forward(order, first_jobs, gate_up_weight, model_ways_cols)
    heads_job.join_weights()
    heads_job.blocks, mlp_blocks = tokens.blocks()
    for job in jobs[1:]:
        job.blocks = mlp_blocks

    def store_last():
        if last_jobs:
            store_feed_forward(order, last_jobs, gate_up_weight, model_ways_cols)

    levels = len(heads_job.bits)
    final = len(jobs) + levels
    early = {}
    for i, bit in enumerate(heads_job.bits):
        early.setdefault(min(levels + 2 + i, final), []).append(spread(bit))
    late = {max(final - 1, *early): [attention, paging]}
    run_jobs(jobs, last_jobs, store_last, early, late)
    hidden = jnp.concatenate([job.result for job in jobs[1:]], axis=1)
    return (held["attended"], hidden, held["kv_cache"])


def solution(mesh):
    data_ways = mesh.shape["dp"]
    placed = (
        P("dp", None),
        P(),
        P(("dp", "mp"), None),
        P("dp", None),
        P(),
        P(("dp", "mp"), None),
        P(),
        P(),
        P(),
    )

    def run(*args):
        return jax.shard_map(
            shards,
            mesh=mesh,
            in_specs=placed,
            out_specs=(P("dp", "mp"), P("dp", "mp"), P("dp", None, "mp")),
            check_vma=False,
        )(*args)

    return run
```
